32 devices in a mesh: blk: 8 (over y, x, core), col: 4 (over z).
Axes of the slice: x: 2, y: 2, z: 4, core: 2. Of those that a mesh axis runs over, the one named last changes fastest.
Arguments:
- documents: bfloat16 [6144, 768], P('blk'), may hold values from -6 to 6
- landmarks: bfloat16 [4096, 768], P(('blk', 'col')), may hold values from -6 to 6
- eigen_vectors: bfloat16 [4096, 256], P(('blk', 'col')), may hold values from -6 to 6
- land_degree: float32 [4096], P(('blk', 'col')), may hold values from 0.5 to 8
- eigen_values: float32 [256], replicated, may hold values from 0.005 to 0.05
- tile_mask: int32 [48, 32], P('blk'), may hold values from 0 to 1, as said below
- labels: int32 [6144], P(('blk', 'col')), may hold values from 0 to 999
Outputs:
- embedding: float32 [6144, 256], P(('blk', 'col'))
- centroids: float32 [1000, 256], replicated
The draws below stay inside these ranges and needn't reach their ends.
Inputs may be any that keep to these rules, and one draw needn't show every extreme that they name: `tile_mask`: 1 marks a live tile of 128 documents by 128 landmarks; every document block has at least one live tile.
All inputs are finite; a program needn't handle non-finite values.
Results may differ from the reference program's by a relative error of at most 0.0041.
Values may be sent and summed in bfloat16 or wider, within the bound.
No kernel may reach another device: no remote copies, remote signals or barrier semaphores. Data moves between devices by JAX's collectives and lax.ppermute only.
A program may use at most 64 MiB of HBM per device.

```python
import math
import jax
import jax.numpy as jnp
from jax import lax

F = 768
K = 256
C = 1000
BLOCK = 128
ND = 6144
NL = 4096


def draw_tile_mask(key, part):
    doc_rows = ND // BLOCK
    land_cols = NL // BLOCK
    base = jax.random.fold_in(key, 17)
    first, second, third = jax.random.split(base, 3)
    level = jax.random.randint(first, (doc_rows, 1), 0, 6)
    coins = jax.random.randint(second, (doc_rows, land_cols), 0, 64)
    alive = coins < jnp.left_shift(jnp.ones_like(level), level)
    forced = jax.random.randint(third, (doc_rows, 1), 0, land_cols)
    struck = jnp.arange(land_cols, dtype=jnp.int32)[None, :] == forced
    return jnp.logical_or(alive, struck).astype(jnp.int32)


def set_ends(array, rng, low, high):
    longest = array.shape.index(max(array.shape))
    spots = []
    for shift in (0, 1):
        where = [jax.random.randint(jax.random.fold_in(rng, axis), (), 0, length) for axis, length in enumerate(array.shape)]
        where[longest] = (where[longest] + shift) % array.shape[longest]
        spots.append(tuple(where))
    return array.at[spots[0]].set(low).at[spots[1]].set(high)


def levels(stream_key, dims, shards, least, high):
    level, own = 1.0, jax.random.fold_in(stream_key, 6)
    for axis_at, parts in shards:
        heights = jnp.exp(jax.random.uniform(jax.random.fold_in(own, axis_at), (parts,), jnp.float32, least / len(shards), high / len(shards)))
        level = level * jnp.repeat(heights, dims[axis_at] // parts).reshape([-1 if axis == axis_at else 1 for axis in range(len(dims))])
    return level


def bell_draw(rng, extent, width, reach, pieces=(), held_as=jnp.bfloat16):
    level = levels(rng, extent, pieces, -0.22, 0.18) if pieces else 1.0
    values = jax.random.normal(rng, extent, jnp.float32) * width * level
    return jnp.minimum(jnp.maximum(values, -reach), reach).astype(held_as)


def setup_inputs(seed: int = 0) -> dict:
    key_list = jax.random.split(jax.random.key(seed), 8)
    return {
        "documents": bell_draw(key_list[0], (ND, F), 1.0, 6.0, ((0, 8),)),
        "landmarks": bell_draw(key_list[1], (NL, F), 1.0, 6.0, ((0, 32),)),
        "eigen_vectors": bell_draw(key_list[2], (NL, K), 1.0, 6.0, ((0, 32),)),
        "land_degree": jnp.clip(jnp.exp(math.log(8.0) - 2.7725887 * jax.random.uniform(key_list[3], (NL,), jnp.float32) ** levels(key_list[3], (NL,), ((0, 32),), -0.2, 0.2)), 0.5, 8.0),
        "eigen_values": jnp.clip(jnp.exp(jax.random.uniform(key_list[4], (K,), jnp.float32, math.log(0.005), math.log(0.05))), 0.005, 0.05),
        "tile_mask": draw_tile_mask(jax.random.fold_in(key_list[7], 71), 0),
        "labels": set_ends(jax.random.randint(key_list[6], (ND,), 0, C), jax.random.fold_in(key_list[6], 1), 0, C - 1).astype(jnp.int32),
    }


def reference(documents, landmarks, eigen_vectors, land_degree, eigen_values, tile_mask, labels):
    inverse_width = 4.0 / F
    scaled = (eigen_vectors.astype(jnp.float32) * lax.rsqrt(land_degree)[:, None] / eigen_values[None, :]).astype(jnp.bfloat16)
    land_blocks = landmarks.reshape(NL // BLOCK, BLOCK, F)
    vector_blocks = scaled.reshape(NL // BLOCK, BLOCK, K)
    land_square = lax.optimization_barrier(jnp.sum(jnp.square(landmarks.astype(jnp.float32)), 1)).reshape(NL // BLOCK, BLOCK)
    doc_blocks = documents.reshape(ND // BLOCK, BLOCK, F)

    def one_block(item):
        doc_block, live_row = item
        doc_square = lax.optimization_barrier(jnp.sum(jnp.square(doc_block.astype(jnp.float32)), 1))

        def step(carry, index):

            def absorb(state):
                land_block = lax.dynamic_index_in_dim(land_blocks, index, 0, keepdims=False)
                vector_block = lax.dynamic_index_in_dim(vector_blocks, index, 0, keepdims=False)
                square_block = lax.dynamic_index_in_dim(land_square, index, 0, keepdims=False)
                products = jnp.einsum('df,lf->dl', doc_block, land_block, preferred_element_type=jnp.float32)
                weights = jnp.exp(inverse_width * (2.0 * products - doc_square[:, None] - square_block[None, :]))
                total = state[0] + jnp.dot(weights.astype(jnp.bfloat16), vector_block, preferred_element_type=jnp.float32)
                return (total, state[1] + lax.optimization_barrier(jnp.sum(weights, 1)))
            live_flag = lax.dynamic_index_in_dim(live_row, index, 0, keepdims=False)
            return (lax.cond(live_flag > 0, absorb, lambda state: state, carry), None)
        initial = (jnp.zeros((BLOCK, K), jnp.float32), jnp.zeros((BLOCK,), jnp.float32))
        result, unused = lax.scan(step, initial, jnp.arange(NL // BLOCK, dtype=jnp.int32))
        return result
    projection, degree = lax.map(one_block, (doc_blocks, tile_mask))
    projection = projection.reshape(ND, K)
    degree = degree.reshape(ND)
    embedding = projection * lax.rsqrt(degree)[:, None]
    unit_rows = embedding * lax.rsqrt(lax.optimization_barrier(jnp.sum(jnp.square(embedding), 1, keepdims=True)) + 1e-06)
    centroids = jax.ops.segment_sum(unit_rows, labels, num_segments=C)
    return (embedding, centroids)
```

```python
import functools

import jax
import jax.numpy as jnp
from jax import lax
from jax.experimental import pallas as pl
from jax.experimental.pallas import tpu as pltpu
from jax.sharding import PartitionSpec as P

C = 1000
BLOCK = 128
TAIL = 16
F32 = jnp.float32
BF16 = jnp.bfloat16


VMEM = pl.BlockSpec(memory_space=pltpu.VMEM)
SMEM = pl.BlockSpec(memory_space=pltpu.SMEM)


def call(kernel, outs, args, specs=None, scratch=(), flops=1000):
    nbytes = sum(a.size * a.dtype.itemsize for a in list(args) + list(outs))
    return pl.pallas_call(
        kernel,
        out_shape=outs,
        in_specs=specs or [VMEM] * len(args),
        out_specs=[VMEM] * len(outs),
        scratch_shapes=list(scratch),
        cost_estimate=pl.CostEstimate(flops=flops, bytes_accessed=nbytes, transcendentals=0),
    )(*args)


def struct(shape, dtype):
    return jax.ShapeDtypeStruct(shape, dtype)


def eye(rows, cols):
    return lax.broadcasted_iota(jnp.int32, (rows, cols), 0) == lax.broadcasted_iota(
        jnp.int32, (rows, cols), 1
    )


def to_row(col, cols):
    n = col.shape[0]
    return jnp.sum(jnp.where(eye(n, cols), jnp.broadcast_to(col, (n, cols)), 0.0), 0, keepdims=True)


def to_col(row, rows):
    n = row.shape[1]
    return jnp.sum(jnp.where(eye(rows, n), jnp.broadcast_to(row, (rows, n)), 0.0), 1, keepdims=True)


def prep_kernel(land_ref, vec_ref, deg_ref, val_ref, out_ref):
    features = land_ref.shape[1]
    out_ref[:, :features] = land_ref[...]
    root = to_col(lax.rsqrt(deg_ref[...]), land_ref.shape[0])
    out_ref[:, features:] = (vec_ref[...].astype(F32) * root / val_ref[...]).astype(BF16)


def square_kernel(doc_ref, out_ref):
    for i in range(doc_ref.shape[0] // BLOCK):
        rows = pl.ds(i * BLOCK, BLOCK)
        block = doc_ref[rows, :].astype(F32)
        total = jnp.sum(block * block, 1, keepdims=True)
        out_ref[rows, :] = jnp.broadcast_to(total, (BLOCK, 128))


def absorb(first, chips, doc_ref, square_ref, mask_ref, pieces, total_ref, degree_ref, prod_ref, low_ref):
    features = doc_ref.shape[1]
    land_rows = pieces[0].shape[0]
    blocks = land_rows // BLOCK
    width = 2 * land_rows
    inverse_width = 4.0 / features
    me = lax.axis_index("blk")
    col = lax.axis_index("col")
    cols = lax.axis_size("col")
    for n, chip in enumerate(chips):
        near, far = pieces[2 * n], pieces[2 * n + 1]
        if chip[0] == chip[1]:
            chip = chip[0]
        else:
            chip = jnp.where(me % 2 == 0, chip[0], chip[1])
        lands = jnp.concatenate([near[:, :features], far[:, :features]], 0)
        vectors = jnp.concatenate([near[:, features:], far[:, features:]], 0)
        wide = lands.astype(F32)
        land_square = to_row(jnp.sum(wide * wide, 1, keepdims=True), width)
        prod_ref[...] = lax.dot_general(
            doc_ref[...], lands, (((1,), (1,)), ((), ())), preferred_element_type=F32
        )
        lane = lax.broadcasted_iota(jnp.int32, (1, width), 1)
        for i in range(doc_ref.shape[0] // BLOCK):
            rows = pl.ds(i * BLOCK, BLOCK)
            live = jnp.zeros((1, width), F32)
            for core in range(2):
                owner = jnp.bitwise_xor(me, 2 * chip + core)
                for j in range(blocks):
                    flag = mask_ref[i, (owner * cols + col) * blocks + j]
                    spot = core * blocks + j
                    here = jnp.logical_and(lane >= spot * BLOCK, lane < (spot + 1) * BLOCK)
                    live = jnp.where(here, flag.astype(F32), live)
            doc_square = square_ref[rows, :][:, :1]
            weights = jnp.exp(inverse_width * (2.0 * prod_ref[rows, :] - doc_square - land_square)) * live
            low_ref[rows, :] = weights.astype(BF16)
            part = weights[:, :128]
            for j in range(1, width // 128):
                part = part + weights[:, j * 128 : (j + 1) * 128]
            if first and n == 0:
                degree_ref[rows, :] = part
            else:
                degree_ref[rows, :] = degree_ref[rows, :] + part
        add = jnp.dot(low_ref[...], vectors, preferred_element_type=F32)
        if first and n == 0:
            total_ref[...] = add
        else:
            total_ref[...] = total_ref[...] + add


def first_kernel(chips, doc_ref, square_ref, mask_ref, *refs):
    pieces, (total_ref, degree_ref, prod_ref, low_ref) = refs[: 2 * len(chips)], refs[2 * len(chips) :]
    absorb(True, chips, doc_ref, square_ref, mask_ref, pieces, total_ref, degree_ref, prod_ref, low_ref)


def more_kernel(chips, doc_ref, square_ref, mask_ref, total_in, degree_in, *refs):
    pieces, (total_ref, degree_ref, prod_ref, low_ref) = refs[: 2 * len(chips)], refs[2 * len(chips) :]
    total_ref[...] = total_in[...]
    degree_ref[...] = degree_in[...]
    absorb(False, chips, doc_ref, square_ref, mask_ref, pieces, total_ref, degree_ref, prod_ref, low_ref)


def last_kernel(chips, doc_ref, square_ref, mask_ref, total_in, degree_in, *refs):
    pieces, refs = refs[: 2 * len(chips)], refs[2 * len(chips) :]
    own_ref, own_deg_ref = refs[:2]
    sends = refs[2:-4]
    prod_ref, low_ref, total_ref, degree_ref = refs[-4:]
    total_ref[...] = total_in[...]
    degree_ref[...] = degree_in[...]
    absorb(False, chips, doc_ref, square_ref, mask_ref, pieces, total_ref, degree_ref, prod_ref, low_ref)
    n, k = own_ref.shape
    col = lax.axis_index("col")
    for mask in range(len(sends) + 1):
        rows = pl.ds(pl.multiple_of(jnp.bitwise_xor(col, mask) * n, 8), n)
        deg = to_row(jnp.sum(degree_ref[rows, :], 1, keepdims=True), k)
        if mask == 0:
            own_ref[...] = total_ref[rows, :]
            own_deg_ref[...] = jnp.broadcast_to(deg, own_deg_ref.shape)
        else:
            out = sends[mask - 1]
            out[:n, :] = total_ref[rows, :].astype(BF16)
            high = deg.astype(BF16).astype(F32)
            spot = lax.broadcasted_iota(jnp.int32, (TAIL, k), 0)
            tail = jnp.where(spot == 0, high, jnp.where(spot == 1, deg - high, 0.0))
            out[n:, :] = tail.astype(BF16)


def norm_kernel(own_ref, own_deg_ref, label_ref, *refs):
    emb_ref, keep_ref, send_ref = refs[-3:]
    gets = refs[:-3]
    n, k = own_ref.shape
    proj = own_ref[...]
    deg = own_deg_ref[:1, :]
    for get in gets:
        proj = proj + get[:n, :].astype(F32)
        tail = get[n:, :].astype(F32)
        deg = deg + (tail[:1, :] + tail[1:2, :])
    emb = proj * lax.rsqrt(to_col(deg, n))
    emb_ref[...] = emb
    unit = emb * lax.rsqrt(jnp.sum(emb * emb, 1, keepdims=True) + 1e-06)
    high = unit.astype(BF16)
    low = (unit - high.astype(F32)).astype(BF16)
    me = lax.axis_index("blk")
    chips = lax.axis_size("blk") // 2
    size = keep_ref.shape[0] // chips
    labels = jnp.broadcast_to(label_ref[...], (size, n))
    spot = lax.broadcasted_iota(jnp.int32, (size, n), 0)
    for core, out in enumerate((keep_ref, send_ref)):
        for chip in range(chips):
            owner = jnp.bitwise_xor(me, 2 * chip + core)
            hot = jnp.where(labels == spot + owner * size, 1.0, 0.0).astype(BF16)
            part = jnp.dot(hot, high, preferred_element_type=F32)
            part = part + jnp.dot(hot, low, preferred_element_type=F32)
            out[chip * size : (chip + 1) * size, :] = part.astype(out.dtype)


def split_kernel(keep_ref, get_ref, own_ref, *sends):
    size = own_ref.shape[0]
    for chip in range(len(sends) + 1):
        rows = slice(chip * size, (chip + 1) * size)
        both = keep_ref[rows, :] + get_ref[rows, :].astype(F32)
        out = sends[chip - 1] if chip else own_ref
        out[...] = both.astype(out.dtype)


def sum_kernel(*refs):
    outs = [r for r in refs[-2:]]
    total = refs[0][...]
    for ref in refs[1:-2]:
        total = total + ref[...].astype(F32)
    for out in outs:
        out[...] = total.astype(out.dtype)


def final_kernel(*refs):
    parts, out_ref, all_ref = refs[:-2], refs[-2], refs[-1]
    me = lax.axis_index("blk")
    size = parts[0].shape[0]
    for n, part in enumerate(parts):
        chip, core = n // 2, n % 2
        owner = jnp.bitwise_xor(me, 2 * chip + core)
        all_ref[pl.ds(pl.multiple_of(owner * size, 8), size), :] = part[...].astype(F32)
    out_ref[...] = all_ref[: out_ref.shape[0], :]


def body(documents, landmarks, eigen_vectors, land_degree, eigen_values, tile_mask, labels):
    blks, cols = lax.axis_size("blk"), lax.axis_size("col")
    chips = blks // 2
    doc_rows, features = documents.shape
    land_rows = landmarks.shape[0]
    k = eigen_vectors.shape[1]
    rows = doc_rows // cols
    assert rows <= k and doc_rows % BLOCK == 0 and land_rows % BLOCK == 0

    def swap(x, pick):
        return lax.ppermute(x, "blk", [(i, pick(i)) for i in range(blks)])

    def core_swap(x):
        return swap(x, lambda i: i ^ 1)

    def chip_swap(x, mask):
        return swap(x, lambda i: i ^ (2 * mask))

    def col_swap(x, mask):
        return lax.ppermute(x, "col", [(i, i ^ mask) for i in range(cols)])

    own = call(
        prep_kernel,
        [struct((land_rows, features + k), BF16)],
        [landmarks, eigen_vectors, land_degree.reshape(1, -1), eigen_values.reshape(1, -1)],
    )[0]
    square = call(square_kernel, [struct((doc_rows, 128), F32)], [documents])[0]

    if chips == 4:
        step_a = lambda i: i ^ 2 if i % 2 == 0 else i ^ 4
        step_b = lambda i: i ^ 4 if i % 2 == 0 else i ^ 2
        got_a = swap(own, step_a)
        got_b = swap(own, step_b)
        own_far = core_swap(own)
        got_f = swap(got_a, step_b)
        a_far, b_far, f_far = core_swap(got_a), core_swap(got_b), core_swap(got_f)
        groups = [[(own, own_far)], [(got_a, b_far), (got_b, a_far)], [(got_f, f_far)]]
        order = [[(0, 0)], [(1, 2), (2, 1)], [(3, 3)]]
    else:
        near = [own] + [chip_swap(own, mask) for mask in range(1, chips)]
        pairs = [(x, core_swap(x)) for x in near]
        groups = [pairs[:1], pairs[1:-1], pairs[-1:]]
        masks = [(mask, mask) for mask in range(chips)]
        order = [masks[:1], masks[1:-1], masks[-1:]]

    scratch = [pltpu.VMEM((doc_rows, 2 * land_rows), F32), pltpu.VMEM((doc_rows, 2 * land_rows), BF16)]
    sums = [struct((doc_rows, k), F32), struct((doc_rows, 128), F32)]
    head = [documents, square, tile_mask]

    def run(kernel, group, masks, outs, extra, scratch):
        pieces = [p for pair in group for p in pair]
        args = head + extra + pieces
        specs = [VMEM, VMEM, SMEM] + [VMEM] * (len(args) - 3)
        flops = len(group) * 4 * doc_rows * land_rows * (features + k)
        return call(functools.partial(kernel, masks), outs, args, specs, scratch, flops)

    state = run(first_kernel, groups[0], order[0], sums, [], scratch)
    state = run(more_kernel, groups[1], order[1], sums, list(state), scratch)
    outs = [struct((rows, k), F32), struct((8, k), F32)]
    outs += [struct((rows + TAIL, k), BF16)] * (cols - 1)
    spare = [pltpu.VMEM((doc_rows, k), F32), pltpu.VMEM((doc_rows, 128), F32)]
    parts = run(last_kernel, groups[2], order[2], outs, list(state), scratch + spare)

    gets = [col_swap(x, mask + 1) for mask, x in enumerate(parts[2:])]
    size = -(-(-(-C // blks)) // TAIL) * TAIL
    embedding, keep, send = call(
        norm_kernel,
        [struct((rows, k), F32), struct((chips * size, k), F32), struct((chips * size, k), BF16)],
        [parts[0], parts[1], labels.reshape(1, -1), *gets],
    )
    get = core_swap(send)
    one, low = struct((size, k), F32), struct((size, k), BF16)
    split = call(split_kernel, [one] + [low] * (chips - 1), [keep, get])
    gets = [chip_swap(x, mask + 1) for mask, x in enumerate(split[1:])]
    mine, mine_low = call(sum_kernel, [one, low], [split[0], *gets])
    gets = [col_swap(mine_low, mask) for mask in range(1, cols)]
    _, done = call(sum_kernel, [one, low], [mine, *gets])
    near = [done] + [chip_swap(done, mask) for mask in range(1, chips)]
    pieces = [p for x in near for p in (x, core_swap(x))]
    centroids = call(
        final_kernel, [struct((C, k), F32)], pieces, scratch=[pltpu.VMEM((blks * size, k), F32)]
    )[0]
    return (embedding, centroids)


def solution(mesh):
    placed = (
        P("blk", None),
        P(("blk", "col"), None),
        P(("blk", "col"), None),
        P(("blk", "col")),
        P(),
        P("blk", None),
        P(("blk", "col")),
    )
    return jax.shard_map(
        body, mesh=mesh, in_specs=placed, out_specs=(P(("blk", "col"), None), P()), check_vma=False
    )
```

```python
import functools

import jax
import jax.numpy as jnp
from jax import lax
from jax.experimental import pallas as pl
from jax.experimental.pallas import tpu as pltpu
from jax.sharding import PartitionSpec as P


C = 1000
BLOCK = 128
TAIL = 16
F32 = jnp.float32
BF16 = jnp.bfloat16


VMEM = pl.BlockSpec(memory_space=pltpu.VMEM)
SMEM = pl.BlockSpec(memory_space=pltpu.SMEM)


def call(kernel, outs, args, specs=None, scratch=(), flops=1000, mib=16):
    nbytes = sum(a.size * a.dtype.itemsize for a in list(args) + list(outs))
    return pl.pallas_call(
        kernel,
        out_shape=outs,
        in_specs=specs or [VMEM] * len(args),
        out_specs=[VMEM] * len(outs),
        scratch_shapes=list(scratch),
        compiler_params=pltpu.CompilerParams(vmem_limit_bytes=mib << 20),
        cost_estimate=pl.CostEstimate(flops=flops, bytes_accessed=nbytes, transcendentals=0),
    )(*args)


def struct(shape, dtype):
    return jax.ShapeDtypeStruct(shape, dtype)


def eye(rows, cols):
    return lax.broadcasted_iota(jnp.int32, (rows, cols), 0) == lax.broadcasted_iota(
        jnp.int32, (rows, cols), 1
    )


def to_row(col, cols):
    n = col.shape[0]
    return jnp.sum(jnp.where(eye(n, cols), jnp.broadcast_to(col, (n, cols)), 0.0), 0, keepdims=True)


def to_col(row, rows):
    n = row.shape[1]
    return jnp.sum(jnp.where(eye(rows, n), jnp.broadcast_to(row, (rows, n)), 0.0), 1, keepdims=True)


def prep_kernel(land_hbm, vec_hbm, deg_hbm, val_hbm, out_ref, vec_ref, deg_ref, val_ref, sem):
    features = land_hbm.shape[1]
    copies = [
        pltpu.make_async_copy(src, dst, sem.at[i])
        for i, (src, dst) in enumerate(
            (
                (land_hbm, out_ref.at[:, :features]),
                (vec_hbm, vec_ref),
                (deg_hbm, deg_ref),
                (val_hbm, val_ref),
            )
        )
    ]
    for copy in copies:
        copy.start()
    for copy in copies[1:]:
        copy.wait()
    root = to_col(lax.rsqrt(deg_ref[...]), vec_ref.shape[0])
    out_ref[:, features:] = (vec_ref[...].astype(F32) * root / val_ref[...]).astype(BF16)
    copies[0].wait()


def square_kernel(doc_ref, out_ref):
    for i in range(doc_ref.shape[0] // BLOCK):
        rows = pl.ds(i * BLOCK, BLOCK)
        block = doc_ref[rows, :].astype(F32)
        total = jnp.sum(block * block, 1, keepdims=True)
        out_ref[rows, :] = jnp.broadcast_to(total, (BLOCK, 128))


def absorb(first, chips, doc_ref, square_ref, mask_ref, pieces, total_ref, degree_ref, prod_ref, low_ref):
    features = doc_ref.shape[1]
    land_rows = pieces[0].shape[0]
    blocks = land_rows // BLOCK
    width = 2 * land_rows
    inverse_width = 4.0 / features
    me = lax.axis_index("blk")
    col = lax.axis_index("col")
    cols = lax.axis_size("col")
    for n, chip in enumerate(chips):
        near, far = pieces[2 * n], pieces[2 * n + 1]
        if chip[0] == chip[1]:
            chip = chip[0]
        else:
            chip = jnp.where(me % 2 == 0, chip[0], chip[1])
        lands = jnp.concatenate([near[:, :features], far[:, :features]], 0)
        vectors = jnp.concatenate([near[:, features:], far[:, features:]], 0)
        wide = lands.astype(F32)
        land_square = to_row(jnp.sum(wide * wide, 1, keepdims=True), width)
        prod_ref[...] = lax.dot_general(
            doc_ref[...], lands, (((1,), (1,)), ((), ())), preferred_element_type=F32
        )
        lane = lax.broadcasted_iota(jnp.int32, (1, width), 1)
        for i in range(doc_ref.shape[0] // BLOCK):
            rows = pl.ds(i * BLOCK, BLOCK)
            live = jnp.zeros((1, width), F32)
            for core in range(2):
                owner = jnp.bitwise_xor(me, 2 * chip + core)
                for j in range(blocks):
                    flag = mask_ref[i, (owner * cols + col) * blocks + j]
                    spot = core * blocks + j
                    here = jnp.logical_and(lane >= spot * BLOCK, lane < (spot + 1) * BLOCK)
                    live = jnp.where(here, flag.astype(F32), live)
            doc_square = square_ref[rows, :][:, :1]
            weights = jnp.exp(inverse_width * (2.0 * prod_ref[rows, :] - doc_square - land_square)) * live
            low_ref[rows, :] = weights.astype(BF16)
            part = weights[:, :128]
            for j in range(1, width // 128):
                part = part + weights[:, j * 128 : (j + 1) * 128]
            if first and n == 0:
                degree_ref[rows, :] = part
            else:
                degree_ref[rows, :] = degree_ref[rows, :] + part
        add = jnp.dot(low_ref[...], vectors, preferred_element_type=F32)
        if first and n == 0:
            total_ref[...] = add
        else:
            total_ref[...] = total_ref[...] + add


def first_kernel(chips, doc_ref, square_ref, mask_ref, *refs):
    pieces, (total_ref, degree_ref, prod_ref, low_ref) = refs[: 2 * len(chips)], refs[2 * len(chips) :]
    absorb(True, chips, doc_ref, square_ref, mask_ref, pieces, total_ref, degree_ref, prod_ref, low_ref)


def more_kernel(chips, doc_ref, square_ref, mask_ref, total_in, degree_in, *refs):
    pieces, (total_ref, degree_ref, prod_ref, low_ref) = refs[: 2 * len(chips)], refs[2 * len(chips) :]
    total_ref[...] = total_in[...]
    degree_ref[...] = degree_in[...]
    absorb(False, chips, doc_ref, square_ref, mask_ref, pieces, total_ref, degree_ref, prod_ref, low_ref)


def last_kernel(chips, doc_ref, square_ref, mask_ref, total_in, degree_in, *refs):
    pieces, refs = refs[: 2 * len(chips)], refs[2 * len(chips) :]
    own_ref, own_deg_ref = refs[:2]
    sends = refs[2:-4]
    prod_ref, low_ref, total_ref, degree_ref = refs[-4:]
    total_ref[...] = total_in[...]
    degree_ref[...] = degree_in[...]
    absorb(False, chips, doc_ref, square_ref, mask_ref, pieces, total_ref, degree_ref, prod_ref, low_ref)
    n, k = own_ref.shape
    col = lax.axis_index("col")
    for mask in range(len(sends) + 1):
        rows = pl.ds(pl.multiple_of(jnp.bitwise_xor(col, mask) * n, 8), n)
        deg = to_row(jnp.sum(degree_ref[rows, :], 1, keepdims=True), k)
        if mask == 0:
            own_ref[...] = total_ref[rows, :]
            own_deg_ref[...] = jnp.broadcast_to(deg, own_deg_ref.shape)
        else:
            out = sends[mask - 1]
            out[:n, :] = total_ref[rows, :].astype(BF16)
            high = deg.astype(BF16).astype(F32)
            spot = lax.broadcasted_iota(jnp.int32, (TAIL, k), 0)
            tail = jnp.where(spot == 0, high, jnp.where(spot == 1, deg - high, 0.0))
            out[n:, :] = tail.astype(BF16)


def norm_kernel(own_ref, own_deg_ref, label_ref, *refs):
    emb_ref, keep_ref, send_ref = refs[-3:]
    gets = refs[:-3]
    n, _ = own_ref.shape
    proj = own_ref[...]
    deg = own_deg_ref[:1, :]
    for get in gets:
        proj = proj + get[:n, :].astype(F32)
        tail = get[n:, :].astype(F32)
        deg = deg + (tail[:1, :] + tail[1:2, :])
    emb = proj * lax.rsqrt(to_col(deg, n))
    emb_ref[...] = emb
    unit = emb * lax.rsqrt(jnp.sum(emb * emb, 1, keepdims=True) + 1e-06)
    high = unit.astype(BF16)
    low = (unit - high.astype(F32)).astype(BF16)
    me = lax.axis_index("blk")
    chips = lax.axis_size("blk") // 2
    size = keep_ref.shape[0] // chips
    labels = jnp.broadcast_to(label_ref[...], (size, n))
    spot = lax.broadcasted_iota(jnp.int32, (size, n), 0)
    for core, out in enumerate((keep_ref, send_ref)):
        for chip in range(chips):
            owner = jnp.bitwise_xor(me, 2 * chip + core)
            hot = jnp.where(labels == spot + owner * size, 1.0, 0.0).astype(BF16)
            part = jnp.dot(hot, high, preferred_element_type=F32)
            part = part + jnp.dot(hot, low, preferred_element_type=F32)
            out[chip * size : (chip + 1) * size, :] = part.astype(out.dtype)


def split_kernel(keep_ref, get_ref, own_ref, *sends):
    size = own_ref.shape[0]
    for chip in range(len(sends) + 1):
        rows = slice(chip * size, (chip + 1) * size)
        both = keep_ref[rows, :] + get_ref[rows, :].astype(F32)
        out = sends[chip - 1] if chip else own_ref
        out[...] = both.astype(out.dtype)


def sum_kernel(*refs):
    outs = [r for r in refs[-2:]]
    total = refs[0][...]
    for ref in refs[1:-2]:
        total = total + ref[...].astype(F32)
    for out in outs:
        out[...] = total.astype(out.dtype)


def final_kernel(*refs):
    parts, out_ref, all_ref = refs[:-2], refs[-2], refs[-1]
    me = lax.axis_index("blk")
    size = parts[0].shape[0]
    for n, part in enumerate(parts):
        chip, core = n // 2, n % 2
        owner = jnp.bitwise_xor(me, 2 * chip + core)
        all_ref[pl.ds(pl.multiple_of(owner * size, 8), size), :] = part[...].astype(F32)
    out_ref[...] = all_ref[: out_ref.shape[0], :]


def body(documents, landmarks, eigen_vectors, land_degree, eigen_values, tile_mask, labels):
    blks, cols = lax.axis_size("blk"), lax.axis_size("col")
    chips = blks // 2
    doc_rows, features = documents.shape
    land_rows = landmarks.shape[0]
    k = eigen_vectors.shape[1]
    rows = doc_rows // cols
    assert rows <= k and doc_rows % BLOCK == 0 and land_rows % BLOCK == 0

    def swap(x, pick):
        return lax.ppermute(x, "blk", [(i, pick(i)) for i in range(blks)])

    def core_swap(x):
        return swap(x, lambda i: i ^ 1)

    def chip_swap(x, mask):
        return swap(x, lambda i: i ^ (2 * mask))

    def col_swap(x, mask):
        return lax.ppermute(x, "col", [(i, i ^ mask) for i in range(cols)])

    own = call(
        prep_kernel,
        [struct((land_rows, features + k), BF16)],
        [landmarks, eigen_vectors, land_degree.reshape(1, -1), eigen_values.reshape(1, -1)],
        [pl.BlockSpec(memory_space=pltpu.HBM)] * 4,
        [
            pltpu.VMEM((land_rows, k), BF16),
            pltpu.VMEM((1, land_rows), F32),
            pltpu.VMEM((1, k), F32),
            pltpu.SemaphoreType.DMA((4,)),
        ],
        mib=60,
    )[0]

    scratch = [pltpu.VMEM((doc_rows, 2 * land_rows), F32), pltpu.VMEM((doc_rows, 2 * land_rows), BF16)]
    sums = [struct((doc_rows, k), F32), struct((doc_rows, 128), F32)]

    def run(kernel, group, masks, outs, extra, scratch):
        pieces = [p for pair in group for p in pair]
        args = [documents, square, tile_mask] + extra + pieces
        specs = [VMEM, VMEM, SMEM] + [VMEM] * (len(args) - 3)
        flops = len(group) * 4 * doc_rows * land_rows * (features + k)
        return call(functools.partial(kernel, masks), outs, args, specs, scratch, flops)

    if chips == 4:
        step_a = lambda i: i ^ 2 if i % 2 == 0 else i ^ 4
        step_b = lambda i: i ^ 4 if i % 2 == 0 else i ^ 2
        got_a = swap(own, step_a)
        got_b = swap(own, step_b)
        got_f = swap(got_a, step_b)
        pairs = [(own, core_swap(own)), (got_a, core_swap(got_b)), (got_b, core_swap(got_a)), (got_f, core_swap(got_f))]
        masks = [(0, 0), (1, 2), (2, 1), (3, 3)]
    else:
        near = [own] + [chip_swap(own, mask) for mask in range(1, chips)]
        pairs = [(x, core_swap(x)) for x in near]
        masks = [(mask, mask) for mask in range(chips)]
    square = call(square_kernel, [struct((doc_rows, 128), F32)], [documents])[0]
    state = run(first_kernel, pairs[:1], masks[:1], sums, [], scratch)
    state = run(more_kernel, pairs[1:-1], masks[1:-1], sums, list(state), scratch)
    last, last_mask = pairs[-1:], masks[-1:]
    outs = [struct((rows, k), F32), struct((8, k), F32)]
    outs += [struct((rows + TAIL, k), BF16)] * (cols - 1)
    spare = [pltpu.VMEM((doc_rows, k), F32), pltpu.VMEM((doc_rows, 128), F32)]
    parts = run(last_kernel, last, last_mask, outs, list(state), scratch + spare)

    gets = [col_swap(x, mask + 1) for mask, x in enumerate(parts[2:])]
    size = -(-(-(-C // blks)) // TAIL) * TAIL
    embedding, keep, send = call(
        norm_kernel,
        [struct((rows, k), F32), struct((chips * size, k), F32), struct((chips * size, k), BF16)],
        [parts[0], parts[1], labels.reshape(1, -1), *gets],
    )
    get = core_swap(send)
    one, low = struct((size, k), F32), struct((size, k), BF16)
    split = call(split_kernel, [one] + [low] * (chips - 1), [keep, get])
    gets = [chip_swap(x, mask + 1) for mask, x in enumerate(split[1:])]
    mine, mine_low = call(sum_kernel, [one, low], [split[0], *gets])
    gets = [col_swap(mine_low, mask) for mask in range(1, cols)]
    _, done = call(sum_kernel, [one, low], [mine, *gets])
    near = [done] + [chip_swap(done, mask) for mask in range(1, chips)]
    pieces = [p for x in near for p in (x, core_swap(x))]
    centroids = call(
        final_kernel, [struct((C, k), F32)], pieces, scratch=[pltpu.VMEM((blks * size, k), F32)]
    )[0]
    return (embedding, centroids)


def solution(mesh):
    placed = (
        P("blk", None),
        P(("blk", "col"), None),
        P(("blk", "col"), None),
        P(("blk", "col")),
        P(),
        P("blk", None),
        P(("blk", "col")),
    )

    return jax.shard_map(body, mesh=mesh, in_specs=placed, out_specs=(P(("blk", "col"), None), P()), check_vma=False)
```

```python
import functools
import math

import jax
import jax.numpy as jnp
from jax import lax
from jax.experimental import pallas as pl
from jax.experimental.pallas import tpu as pltpu
from jax.sharding import PartitionSpec as P


C = 1000
BLOCK = 128
TAIL = 8
HEAVY = 5_000_000_000
DEAD = 1e30
LOG2E = 1.4426950408889634
F32 = jnp.float32
BF16 = jnp.bfloat16


VMEM = pl.BlockSpec(memory_space=pltpu.VMEM)
SMEM = pl.BlockSpec(memory_space=pltpu.SMEM)


def call(kernel, outs, args, specs=None, scratch=(), flops=1000, mib=16, aliases=None, out_specs=None):
    nbytes = sum(a.size * a.dtype.itemsize for a in list(args) + list(outs))
    return pl.pallas_call(
        kernel,
        out_shape=outs,
        in_specs=specs or [VMEM] * len(args),
        out_specs=out_specs or [VMEM] * len(outs),
        scratch_shapes=list(scratch),
        input_output_aliases=aliases or {},
        compiler_params=pltpu.CompilerParams(vmem_limit_bytes=mib << 20),
        cost_estimate=pl.CostEstimate(flops=flops, bytes_accessed=nbytes, transcendentals=0),
    )(*args)


def struct(shape, dtype):
    return jax.ShapeDtypeStruct(shape, dtype)


def eye(rows, cols):
    return lax.broadcasted_iota(jnp.int32, (rows, cols), 0) == lax.broadcasted_iota(
        jnp.int32, (rows, cols), 1
    )


def to_row(col, cols):
    n = col.shape[0]
    return jnp.sum(jnp.where(eye(n, cols), jnp.broadcast_to(col, (n, cols)), 0.0), 0, keepdims=True)


def to_col(row, rows):
    n = row.shape[1]
    return jnp.sum(jnp.where(eye(rows, n), jnp.broadcast_to(row, (rows, n)), 0.0), 1, keepdims=True)


def spot_kernel(out_ref):
    out_ref[...] = lax.broadcasted_iota(jnp.int32, out_ref.shape, 1)


def prep_kernel(spot_ref, land_ref, vec_ref, deg_ref, val_ref, out_ref):
    features = land_ref.shape[1]
    rows = land_ref.shape[0]
    out_ref[:, :features] = land_ref[...]
    here = lax.broadcasted_iota(jnp.int32, (rows, rows), 0) == spot_ref[:1, :]
    root = jnp.sum(
        jnp.where(here, jnp.broadcast_to(lax.rsqrt(deg_ref[...]), (rows, rows)), 0.0), 1, keepdims=True
    )
    out_ref[:, features:] = (vec_ref[...].astype(F32) * root / val_ref[...]).astype(BF16)


def owner_of(place):
    me = lax.axis_index("blk")
    even, odd = place
    return jnp.bitwise_xor(me, even if even == odd else jnp.where(me % 2 == 0, even, odd))


def weigh(places, doc_ref, square_ref, mask_ref, pieces, low_ref, window, add_degree, add_total):
    base, count, step = window
    features = doc_ref.shape[1]
    land_rows = pieces[0].shape[0]
    blocks = land_rows // BLOCK
    width = len(pieces) * land_rows
    scale = 4.0 / features * LOG2E
    col = lax.axis_index("col")
    cols = lax.axis_size("col")
    lands = jnp.concatenate([p[:, :features] for p in pieces], 0)
    vectors = jnp.concatenate([p[:, features:] for p in pieces], 0)
    wide = lands.astype(F32)
    land_square = scale * to_row(jnp.sum(wide * wide, 1, keepdims=True), width)
    spot = lax.broadcasted_iota(jnp.int32, (1, width), 1) // BLOCK
    owners = [owner_of(place) for place in places]
    whole = pl.ds(base, count)
    prod = lax.dot_general(doc_ref[whole, :], lands, (((1,), (1,)), ((), ())), preferred_element_type=F32)
    for start in range(0, count, step):
        rows, local = pl.ds(base + start, step), slice(start, start + step)
        block = (base + start) // BLOCK
        flags = jnp.zeros((1, width), jnp.int32)
        for n, owner in enumerate(owners):
            for j in range(blocks):
                flag = mask_ref[block, (owner * cols + col) * blocks + j]
                flags = jnp.where(spot == n * blocks + j, flag, flags)
        less = jnp.where(flags > 0, land_square, DEAD)
        weights = jnp.exp2((2.0 * scale) * prod[local] - square_ref[rows, :][:, :1] - less)
        low_ref[local, :width] = weights.astype(BF16)
        part = weights[:, :128]
        for j in range(1, width // 128):
            part = part + weights[:, j * 128 : (j + 1) * 128]
        add_degree(rows, local, part)
    add_total(whole, jnp.dot(low_ref[:count, :width], vectors, preferred_element_type=F32))


def first_kernel(places, doc_ref, mask_ref, *refs):
    pieces, (total_ref, degree_ref, square_ref, low_ref) = refs[:-4], refs[-4:]
    scale = 4.0 / doc_ref.shape[1] * LOG2E
    for i in range(doc_ref.shape[0] // BLOCK):
        rows = pl.ds(i * BLOCK, BLOCK)
        block = doc_ref[rows, :].astype(F32)
        total = scale * jnp.sum(block * block, 1, keepdims=True)
        square_ref[rows, :] = jnp.broadcast_to(total, (BLOCK, 128))

    def add_degree(rows, local, part):
        degree_ref[rows, :] = part

    def add_total(rows, part):
        total_ref[rows, :] = part

    window = 0, doc_ref.shape[0], BLOCK
    weigh(places, doc_ref, square_ref, mask_ref, pieces, low_ref, window, add_degree, add_total)


def more_kernel(places, doc_ref, square_ref, mask_ref, total_in, degree_in, *refs):
    pieces, (total_ref, degree_ref, low_ref) = refs[:-3], refs[-3:]

    def add_degree(rows, local, part):
        degree_ref[rows, :] = degree_in[rows, :] + part

    def add_total(rows, part):
        total_ref[rows, :] = total_in[rows, :] + part

    window = 0, doc_ref.shape[0], BLOCK
    weigh(places, doc_ref, square_ref, mask_ref, pieces, low_ref, window, add_degree, add_total)


def part_kernel(mask, places, doc_ref, square_ref, mask_ref, total_in, degree_in, *refs):
    pieces, refs = refs[: len(places)], refs[len(places) :]
    outs, (low_ref, part_ref) = refs[:-2], refs[-2:]
    n, k = low_ref.shape[0], total_in.shape[1]
    step = math.gcd(n, BLOCK)
    base = pl.multiple_of(jnp.bitwise_xor(lax.axis_index("col"), mask) * n, step)
    totals = []

    def add_degree(rows, local, part):
        part_ref[local, :] = degree_in[rows, :] + part

    def add_total(rows, part):
        totals.append(total_in[rows, :] + part)

    window = base, n, step
    weigh(places, doc_ref, square_ref, mask_ref, pieces, low_ref, window, add_degree, add_total)
    deg = to_row(jnp.sum(part_ref[...], 1, keepdims=True), k)
    if mask == 0:
        outs[0][...] = totals[0]
        outs[1][...] = jnp.broadcast_to(deg, outs[1].shape)
    else:
        outs[0][:n, :] = totals[0].astype(BF16)
        high = deg.astype(BF16).astype(F32)
        spot = lax.broadcasted_iota(jnp.int32, (TAIL, k), 0)
        tail = jnp.where(spot == 0, high, jnp.where(spot == 1, deg - high, 0.0))
        outs[0][n:, :] = tail.astype(BF16)


def embed(own_ref, own_deg_ref, gets):
    n = own_ref.shape[0]
    proj = own_ref[...]
    deg = own_deg_ref[:1, :]
    for get in gets:
        proj = proj + get[:n, :].astype(F32)
        tail = get[n:, :].astype(F32)
        deg = deg + (tail[:1, :] + tail[1:2, :])
    return proj * lax.rsqrt(to_col(deg, n))


def embed_kernel(own_ref, own_deg_ref, *refs):
    refs[-1][...] = embed(own_ref, own_deg_ref, refs[:-1])


def gather_rows(core, label_ref, high, low, out_ref):
    me = lax.axis_index("blk")
    chips = lax.axis_size("blk") // 2
    n = high.shape[0]
    size = out_ref.shape[0] // chips
    labels = jnp.broadcast_to(label_ref[...], (size, n))
    spot = lax.broadcasted_iota(jnp.int32, (size, n), 0)
    for chip in range(chips):
        owner = jnp.bitwise_xor(me, 2 * chip + core)
        hot = jnp.where(labels == spot + owner * size, 1.0, 0.0).astype(BF16)
        part = jnp.dot(hot, high, preferred_element_type=F32)
        part = part + jnp.dot(hot, low, preferred_element_type=F32)
        out_ref[chip * size : (chip + 1) * size, :] = part.astype(out_ref.dtype)


def norm_kernel(own_ref, own_deg_ref, label_ref, *refs):
    send_ref, high_ref, low_ref = refs[-3:]
    emb = embed(own_ref, own_deg_ref, refs[:-3])
    unit = emb * lax.rsqrt(jnp.sum(emb * emb, 1, keepdims=True) + 1e-06)
    high = unit.astype(BF16)
    low = (unit - high.astype(F32)).astype(BF16)
    high_ref[...] = high
    low_ref[...] = low
    gather_rows(1, label_ref, high, low, send_ref)


def keep_kernel(label_ref, high_ref, low_ref, keep_ref):
    gather_rows(0, label_ref, high_ref[...], low_ref[...], keep_ref)


def split_kernel(keep_ref, get_ref, own_ref, *sends):
    size = own_ref.shape[0]
    for chip in range(len(sends) + 1):
        rows = slice(chip * size, (chip + 1) * size)
        both = keep_ref[rows, :] + get_ref[rows, :].astype(F32)
        out = sends[chip - 1] if chip else own_ref
        out[...] = both.astype(out.dtype)


def sum_kernel(count, *refs):
    total = refs[0][...]
    for ref in refs[1:count]:
        total = total + ref[...].astype(F32)
    for out in refs[count:]:
        out[...] = total.astype(out.dtype)


def place_kernel(places, aliased, *refs):
    parts, (out_hbm, wide_ref, sem) = refs[: len(places)], refs[-3:]
    del aliased
    size = parts[0].shape[0]
    count = out_hbm.shape[0]
    whole, rest = count // size, count % size
    copies = []
    for n, (place, part) in enumerate(zip(places, parts)):
        owner = jnp.bitwise_xor(lax.axis_index("blk"), place)
        wide_ref[n] = part[...].astype(F32)
        full = pltpu.make_async_copy(
            wide_ref.at[n],
            out_hbm.at[pl.ds(pl.multiple_of(jnp.minimum(owner, whole - 1) * size, 8), size), :],
            sem.at[n],
        )
        copies.append((owner < whole, full))
        if rest:
            end = pltpu.make_async_copy(
                wide_ref.at[n, pl.ds(0, rest), :], out_hbm.at[pl.ds(whole * size, rest), :], sem.at[n]
            )
            copies.append((owner == whole, end))
    for here, copy in copies:
        pl.when(here)(copy.start)
    for here, copy in copies:
        pl.when(here)(copy.wait)


def body(documents, landmarks, eigen_vectors, land_degree, eigen_values, tile_mask, labels):
    blks, cols = lax.axis_size("blk"), lax.axis_size("col")
    chips = blks // 2
    doc_rows, features = documents.shape
    land_rows = landmarks.shape[0]
    k = eigen_vectors.shape[1]
    rows = doc_rows // cols
    assert rows <= k and doc_rows % BLOCK == 0 and land_rows % BLOCK == 0

    def swap(x, pick):
        return lax.ppermute(x, "blk", [(i, pick(i)) for i in range(blks)])

    def core_swap(x):
        return swap(x, lambda i: i ^ 1)

    def chip_swap(x, mask):
        return swap(x, lambda i: i ^ (2 * mask))

    def col_swap(x, mask):
        return lax.ppermute(x, "col", [(i, i ^ mask) for i in range(cols)])

    spot = call(spot_kernel, [struct((8, land_rows), jnp.int32)], [], flops=HEAVY)[0]
    own = call(
        prep_kernel,
        [struct((land_rows, features + k), BF16)],
        [spot, landmarks, eigen_vectors, land_degree.reshape(1, -1), eigen_values.reshape(1, -1)],
        flops=HEAVY,
    )[0]

    if chips == 4:
        step_a = lambda i: i ^ 2 if i % 2 == 0 else i ^ 4
        step_b = lambda i: i ^ 4 if i % 2 == 0 else i ^ 2
        got_a = swap(own, step_a)
        got_b = swap(own, step_b)
        got_f = swap(got_a, step_b)
        far_own = core_swap(own)
        far_a, far_b, far_f = core_swap(got_a), core_swap(got_b), core_swap(got_f)
        groups = [
            [(own, (0, 0)), (far_own, (1, 1))],
            [(got_a, (2, 4)), (far_a, (5, 3))],
            [(got_b, (4, 2)), (far_b, (3, 5))],
            [(got_f, (6, 6)), (far_f, (7, 7))],
        ]
    else:
        near = [own] + [chip_swap(own, mask) for mask in range(1, chips)]
        groups = [
            [(x, (2 * mask, 2 * mask)), (core_swap(x), (2 * mask + 1, 2 * mask + 1))]
            for mask, x in enumerate(near)
        ]

    scratch = [pltpu.VMEM((doc_rows, 2 * land_rows), BF16)]
    sums = [struct((doc_rows, k), F32), struct((doc_rows, 128), F32)]

    def run(kernel, group, outs, args, scratch, aliases=None, share=1):
        places = [place for _, place in group]
        args = args + [piece for piece, _ in group]
        specs = [SMEM if a is tile_mask else VMEM for a in args]
        flops = len(group) * 2 * doc_rows * land_rows * (features + k) // share
        kernel = functools.partial(kernel, places)
        return call(kernel, outs, args, specs, scratch, flops, aliases=aliases)

    *state, square = run(first_kernel, groups[0], sums + sums[1:], [documents, tile_mask], scratch)
    head = [documents, square, tile_mask]
    for group in groups[1:-1]:
        state = run(more_kernel, group, sums, head + list(state), scratch, {3: 0, 4: 1})
    narrow = [pltpu.VMEM((rows, len(groups[-1]) * land_rows), BF16), pltpu.VMEM((rows, 128), F32)]

    def part(mask, outs):
        kernel = functools.partial(part_kernel, mask)
        return run(kernel, groups[-1], outs, head + list(state), narrow, share=cols)

    parts = part(0, [struct((rows, k), F32), struct((8, k), F32)])
    sends = [part(mask, [struct((rows + TAIL, k), BF16)])[0] for mask in range(1, cols)]
    gets = [col_swap(x, mask + 1) for mask, x in enumerate(sends)]
    size = -(-(-(-C // blks)) // 16) * 16
    names = labels.reshape(1, -1)
    wide, half = struct((chips * size, k), F32), struct((chips * size, k), BF16)
    unit = struct((rows, k), BF16)
    send, high, low = call(norm_kernel, [half, unit, unit], [parts[0], parts[1], names, *gets])
    get = core_swap(send)
    keep = call(keep_kernel, [wide], [names, high, low])[0]
    embedding = call(embed_kernel, [struct((rows, k), F32)], [parts[0], parts[1], *gets])[0]
    one, low = struct((size, k), F32), struct((size, k), BF16)
    split = call(split_kernel, [one] + [low] * (chips - 1), [keep, get])
    gets = [chip_swap(x, mask + 1) for mask, x in enumerate(split[1:])]
    mine, mine_low = call(functools.partial(sum_kernel, chips), [one, low], [split[0], *gets])
    gets = [col_swap(mine_low, mask) for mask in range(1, cols)]
    done = call(functools.partial(sum_kernel, cols), [low], [mine, *gets])[0]
    near = [done] + [chip_swap(done, mask) for mask in range(1, chips)]
    far = [core_swap(x) for x in near]
    centroids = None
    hbm = pl.BlockSpec(memory_space=pl.ANY)
    for core, chunks in enumerate((near, far)):
        extra = [] if centroids is None else [centroids]
        centroids = call(
            functools.partial(place_kernel, [2 * mask + core for mask in range(chips)], bool(extra)),
            [struct((C, k), F32)],
            chunks + extra,
            [VMEM] * chips + [hbm] * len(extra),
            [pltpu.VMEM((chips, size, k), F32), pltpu.SemaphoreType.DMA((chips,))],
            aliases={chips: 0} if extra else None,
            out_specs=[hbm],
        )[0]
    return (embedding, centroids)


def solution(mesh):
    placed = (
        P("blk", None),
        P(("blk", "col"), None),
        P(("blk", "col"), None),
        P(("blk", "col")),
        P(),
        P("blk", None),
        P(("blk", "col")),
    )

    return jax.shard_map(body, mesh=mesh, in_specs=placed, out_specs=(P(("blk", "col"), None), P()), check_vma=False)
```

```python
import functools
import math

import jax
import jax.numpy as jnp
from jax import lax
from jax.experimental import pallas as pl
from jax.experimental.pallas import tpu as pltpu
from jax.sharding import PartitionSpec as P


C = 1000
BLOCK = 128
TAIL = 8
HEAVY = 5_000_000_000
DEAD = 1e30
LOG2E = 1.4426950408889634
F32 = jnp.float32
BF16 = jnp.bfloat16


VMEM = pl.BlockSpec(memory_space=pltpu.VMEM)


def call(kernel, outs, args, specs=None, scratch=(), flops=1000, mib=16, aliases=None, out_specs=None):
    nbytes = sum(a.size * a.dtype.itemsize for a in list(args) + list(outs))
    return pl.pallas_call(
        kernel,
        out_shape=outs,
        in_specs=specs or [VMEM] * len(args),
        out_specs=out_specs or [VMEM] * len(outs),
        scratch_shapes=list(scratch),
        input_output_aliases=aliases or {},
        compiler_params=pltpu.CompilerParams(vmem_limit_bytes=mib << 20),
        cost_estimate=pl.CostEstimate(flops=flops, bytes_accessed=nbytes, transcendentals=0),
    )(*args)


def struct(shape, dtype):
    return jax.ShapeDtypeStruct(shape, dtype)


def eye(rows, cols):
    return lax.broadcasted_iota(jnp.int32, (rows, cols), 0) == lax.broadcasted_iota(
        jnp.int32, (rows, cols), 1
    )


def to_row(col, cols):
    n = col.shape[0]
    return jnp.sum(jnp.where(eye(n, cols), jnp.broadcast_to(col, (n, cols)), 0.0), 0, keepdims=True)


def to_col(row, rows):
    n = row.shape[1]
    return jnp.sum(jnp.where(eye(rows, n), jnp.broadcast_to(row, (rows, n)), 0.0), 1, keepdims=True)


def spot_kernel(out_ref):
    out_ref[...] = lax.broadcasted_iota(jnp.int32, out_ref.shape, 1)


def prep_kernel(spot_ref, land_ref, vec_ref, deg_ref, val_ref, out_ref):
    features = land_ref.shape[1]
    rows = land_ref.shape[0]
    for start in range(0, features, rows):
        part = land_ref[:, start : start + rows]
        out_ref[:, start : start + rows] = part.T
    here = lax.broadcasted_iota(jnp.int32, (rows, rows), 0) == spot_ref[:1, :]
    root = jnp.sum(
        jnp.where(here, jnp.broadcast_to(lax.rsqrt(deg_ref[...]), (rows, rows)), 0.0), 1, keepdims=True
    )
    out_ref[:, features:] = (vec_ref[...].astype(F32) * root / val_ref[...]).astype(BF16)


def owner_of(place):
    me = lax.axis_index("blk")
    even, odd = place
    return jnp.bitwise_xor(me, even if even == odd else jnp.where(me % 2 == 0, even, odd))


def weigh(places, doc_ref, square_ref, mask_ref, pieces, low_ref, window, add_degree, add_total):
    base, count, step = window
    features = doc_ref.shape[1]
    land_rows = pieces[0].shape[0]
    width = len(pieces) * land_rows
    scale = 4.0 / features * LOG2E
    col = lax.axis_index("col")
    cols = lax.axis_size("col")
    lands = jnp.concatenate(
        [
            jnp.concatenate([p[:, start : start + land_rows] for p in pieces], 1)
            for start in range(0, features, land_rows)
        ],
        0,
    )
    vectors = jnp.concatenate([p[:, features:] for p in pieces], 0)
    wide = lands.astype(F32)
    land_square = scale * jnp.sum(wide * wide, 0, keepdims=True)
    live = mask_ref[...].astype(F32)
    lane = lax.broadcasted_iota(jnp.int32, live.shape, 1)
    line = lax.broadcasted_iota(jnp.int32, (live.shape[0], 1), 0)
    flags = [
        jnp.sum(jnp.where(lane == owner_of(place) * cols + col, live, 0.0), 1, keepdims=True)
        for place in places
    ]
    whole = pl.ds(base, count)
    prod = jnp.dot(doc_ref[whole, :], lands, preferred_element_type=F32)
    for start in range(0, count, step):
        rows, local = pl.ds(base + start, step), slice(start, start + step)
        block = (base + start) // BLOCK
        less = jnp.concatenate(
            [
                jnp.where(
                    jnp.sum(jnp.where(line == block, flag, 0.0), 0, keepdims=True) > 0.0,
                    land_square[:, n * land_rows : (n + 1) * land_rows],
                    DEAD,
                )
                for n, flag in enumerate(flags)
            ],
            1,
        )
        weights = jnp.exp2((2.0 * scale) * prod[local] - square_ref[rows, :][:, :1] - less)
        low_ref[local, :width] = weights.astype(BF16)
        part = weights[:, :128]
        for j in range(1, width // 128):
            part = part + weights[:, j * 128 : (j + 1) * 128]
        add_degree(rows, local, part)
    add_total(whole, jnp.dot(low_ref[:count, :width], vectors, preferred_element_type=F32))


def first_kernel(places, doc_ref, mask_ref, *refs):
    pieces, (total_ref, degree_ref, square_ref, low_ref) = refs[:-4], refs[-4:]
    scale = 4.0 / doc_ref.shape[1] * LOG2E
    for i in range(doc_ref.shape[0] // BLOCK):
        rows = pl.ds(i * BLOCK, BLOCK)
        block = doc_ref[rows, :].astype(F32)
        total = scale * jnp.sum(block * block, 1, keepdims=True)
        square_ref[rows, :] = jnp.broadcast_to(total, (BLOCK, 128))

    def add_degree(rows, local, part):
        degree_ref[rows, :] = part

    def add_total(rows, part):
        total_ref[rows, :] = part

    window = 0, doc_ref.shape[0], BLOCK
    weigh(places, doc_ref, square_ref, mask_ref, pieces, low_ref, window, add_degree, add_total)


def more_kernel(places, doc_ref, square_ref, mask_ref, total_in, degree_in, *refs):
    pieces, (total_ref, degree_ref, low_ref) = refs[:-3], refs[-3:]

    def add_degree(rows, local, part):
        degree_ref[rows, :] = degree_in[rows, :] + part

    def add_total(rows, part):
        total_ref[rows, :] = total_in[rows, :] + part

    window = 0, doc_ref.shape[0], BLOCK
    weigh(places, doc_ref, square_ref, mask_ref, pieces, low_ref, window, add_degree, add_total)


def part_kernel(mask, places, doc_ref, square_ref, mask_ref, total_in, degree_in, *refs):
    pieces, refs = refs[: len(places)], refs[len(places) :]
    outs, (low_ref, part_ref) = refs[:-2], refs[-2:]
    n, k = low_ref.shape[0], total_in.shape[1]
    step = math.gcd(n, BLOCK)
    base = pl.multiple_of(jnp.bitwise_xor(lax.axis_index("col"), mask) * n, step)
    totals = []

    def add_degree(rows, local, part):
        part_ref[local, :] = degree_in[rows, :] + part

    def add_total(rows, part):
        totals.append(total_in[rows, :] + part)

    window = base, n, step
    weigh(places, doc_ref, square_ref, mask_ref, pieces, low_ref, window, add_degree, add_total)
    deg = to_row(jnp.sum(part_ref[...], 1, keepdims=True), k)
    if mask == 0:
        outs[0][...] = totals[0]
        outs[1][...] = jnp.broadcast_to(deg, outs[1].shape)
    else:
        outs[0][:n, :] = totals[0].astype(BF16)
        high = deg.astype(BF16).astype(F32)
        spot = lax.broadcasted_iota(jnp.int32, (TAIL, k), 0)
        tail = jnp.where(spot == 0, high, jnp.where(spot == 1, deg - high, 0.0))
        outs[0][n:, :] = tail.astype(BF16)


def embed(own_ref, own_deg_ref, gets):
    n = own_ref.shape[0]
    proj = own_ref[...]
    deg = own_deg_ref[:1, :]
    for get in gets:
        proj = proj + get[:n, :].astype(F32)
        tail = get[n:, :].astype(F32)
        deg = deg + (tail[:1, :] + tail[1:2, :])
    return proj * lax.rsqrt(to_col(deg, n))


def embed_kernel(own_ref, own_deg_ref, *refs):
    refs[-1][...] = embed(own_ref, own_deg_ref, refs[:-1])


def gather_rows(core, label_ref, high, low, out_ref):
    me = lax.axis_index("blk")
    chips = lax.axis_size("blk") // 2
    n = high.shape[0]
    size = out_ref.shape[0] // chips
    labels = jnp.broadcast_to(label_ref[...], (size, n))
    spot = lax.broadcasted_iota(jnp.int32, (size, n), 0)
    for chip in range(chips):
        owner = jnp.bitwise_xor(me, 2 * chip + core)
        hot = jnp.where(labels == spot + owner * size, 1.0, 0.0).astype(BF16)
        part = jnp.dot(hot, high, preferred_element_type=F32)
        part = part + jnp.dot(hot, low, preferred_element_type=F32)
        out_ref[chip * size : (chip + 1) * size, :] = part.astype(out_ref.dtype)


def norm_kernel(own_ref, own_deg_ref, label_ref, *refs):
    send_ref, high_ref, low_ref = refs[-3:]
    emb = embed(own_ref, own_deg_ref, refs[:-3])
    unit = emb * lax.rsqrt(jnp.sum(emb * emb, 1, keepdims=True) + 1e-06)
    high = unit.astype(BF16)
    low = (unit - high.astype(F32)).astype(BF16)
    high_ref[...] = high
    low_ref[...] = low
    gather_rows(1, label_ref, high, low, send_ref)


def keep_kernel(label_ref, high_ref, low_ref, keep_ref):
    gather_rows(0, label_ref, high_ref[...], low_ref[...], keep_ref)


def split_kernel(keep_ref, get_ref, own_ref, *sends):
    size = own_ref.shape[0]
    for chip in range(len(sends) + 1):
        rows = slice(chip * size, (chip + 1) * size)
        both = keep_ref[rows, :] + get_ref[rows, :].astype(F32)
        out = sends[chip - 1] if chip else own_ref
        out[...] = both.astype(out.dtype)


def tree(parts):
    while len(parts) > 1:
        parts = [a + b for a, b in zip(parts[::2], parts[1::2])]
    return parts[0]


def sum_kernel(*refs):
    refs[-1][...] = tree([ref[...].astype(F32) for ref in refs[:-1]]).astype(refs[-1].dtype)


def place_kernel(places, aliased, *refs):
    parts, (out_hbm, wide_ref, sem) = refs[: len(places)], refs[-3:]
    del aliased
    size = parts[0].shape[0]
    count = out_hbm.shape[0]
    whole, rest = count // size, count % size
    copies = []
    for n, (place, part) in enumerate(zip(places, parts)):
        owner = jnp.bitwise_xor(lax.axis_index("blk"), place)
        wide_ref[n] = part[...].astype(F32)
        full = pltpu.make_async_copy(
            wide_ref.at[n],
            out_hbm.at[pl.ds(pl.multiple_of(jnp.minimum(owner, whole - 1) * size, 8), size), :],
            sem.at[n],
        )
        copies.append((owner < whole, full))
        if rest:
            end = pltpu.make_async_copy(
                wide_ref.at[n, pl.ds(0, rest), :], out_hbm.at[pl.ds(whole * size, rest), :], sem.at[n]
            )
            copies.append((owner == whole, end))
    for here, copy in copies:
        pl.when(here)(copy.start)
    for here, copy in copies:
        pl.when(here)(copy.wait)


def body(documents, landmarks, eigen_vectors, land_degree, eigen_values, tile_mask, labels):
    blks, cols = lax.axis_size("blk"), lax.axis_size("col")
    chips = blks // 2
    doc_rows, features = documents.shape
    land_rows = landmarks.shape[0]
    k = eigen_vectors.shape[1]
    rows = doc_rows // cols
    assert rows <= k and doc_rows % BLOCK == 0 and land_rows == BLOCK and features % BLOCK == 0

    def swap(x, pick):
        return lax.ppermute(x, "blk", [(i, pick(i)) for i in range(blks)])

    def core_swap(x):
        return swap(x, lambda i: i ^ 1)

    def chip_swap(x, mask):
        return swap(x, lambda i: i ^ (2 * mask))

    def col_swap(x, mask):
        return lax.ppermute(x, "col", [(i, i ^ mask) for i in range(cols)])

    spot = call(spot_kernel, [struct((8, land_rows), jnp.int32)], [], flops=HEAVY)[0]
    own = call(
        prep_kernel,
        [struct((land_rows, features + k), BF16)],
        [spot, landmarks, eigen_vectors, land_degree.reshape(1, -1), eigen_values.reshape(1, -1)],
        flops=HEAVY,
    )[0]

    if chips == 4:
        step_a = lambda i: i ^ 2 if i % 2 == 0 else i ^ 4
        step_b = lambda i: i ^ 4 if i % 2 == 0 else i ^ 2
        got_a = swap(own, step_a)
        got_b = swap(own, step_b)
        got_f = swap(got_a, step_b)
        far_own = core_swap(own)
        far_a, far_b, far_f = core_swap(got_a), core_swap(got_b), core_swap(got_f)
        groups = [
            [(own, (0, 0)), (far_own, (1, 1))],
            [(got_a, (2, 4)), (far_a, (5, 3))],
            [(got_b, (4, 2)), (far_b, (3, 5))],
            [(got_f, (6, 6)), (far_f, (7, 7))],
        ]
    else:
        near = [own] + [chip_swap(own, mask) for mask in range(1, chips)]
        groups = [
            [(x, (2 * mask, 2 * mask)), (core_swap(x), (2 * mask + 1, 2 * mask + 1))]
            for mask, x in enumerate(near)
        ]

    scratch = [pltpu.VMEM((doc_rows, 2 * land_rows), BF16)]
    sums = [struct((doc_rows, k), F32), struct((doc_rows, 128), F32)]

    def run(kernel, group, outs, args, scratch, aliases=None, share=1):
        places = [place for _, place in group]
        args = args + [piece for piece, _ in group]
        flops = len(group) * 2 * doc_rows * land_rows * (features + k) // share
        kernel = functools.partial(kernel, places)
        return call(kernel, outs, args, None, scratch, flops, aliases=aliases)

    *state, square = run(first_kernel, groups[0], sums + sums[1:], [documents, tile_mask], scratch)
    head = [documents, square, tile_mask]
    for group in groups[1:-1]:
        state = run(more_kernel, group, sums, head + list(state), scratch, {3: 0, 4: 1})
    narrow = [pltpu.VMEM((rows, len(groups[-1]) * land_rows), BF16), pltpu.VMEM((rows, 128), F32)]

    def part(mask, outs):
        kernel = functools.partial(part_kernel, mask)
        return run(kernel, groups[-1], outs, head + list(state), narrow, share=cols)

    parts = part(0, [struct((rows, k), F32), struct((8, k), F32)])
    sends = [part(mask, [struct((rows + TAIL, k), BF16)])[0] for mask in range(1, cols)]
    gets = [col_swap(x, mask + 1) for mask, x in enumerate(sends)]
    size = -(-(-(-C // blks)) // 16) * 16
    names = labels.reshape(1, -1)
    wide, half = struct((chips * size, k), F32), struct((chips * size, k), BF16)
    unit = struct((rows, k), BF16)
    send, high, low = call(norm_kernel, [half, unit, unit], [parts[0], parts[1], names, *gets])
    get = core_swap(send)
    keep = call(keep_kernel, [wide], [names, high, low])[0]
    embedding = call(embed_kernel, [struct((rows, k), F32)], [parts[0], parts[1], *gets])[0]
    one, low = struct((size, k), F32), struct((size, k), BF16)
    split = call(split_kernel, [one] + [low] * (chips - 1), [keep, get])
    gets = [chip_swap(x, mask + 1) for mask, x in enumerate(split[1:])]
    mine = call(sum_kernel, [low], [split[0], *gets])[0]
    gets = [col_swap(mine, mask) for mask in range(1, cols)]
    done = call(sum_kernel, [low], [mine, *gets])[0]
    near = [done] + [chip_swap(done, mask) for mask in range(1, chips)]
    far = [core_swap(x) for x in near]
    centroids = None
    hbm = pl.BlockSpec(memory_space=pl.ANY)
    for core, chunks in enumerate((near, far)):
        extra = [] if centroids is None else [centroids]
        centroids = call(
            functools.partial(place_kernel, [2 * mask + core for mask in range(chips)], bool(extra)),
            [struct((C, k), F32)],
            chunks + extra,
            [VMEM] * chips + [hbm] * len(extra),
            [pltpu.VMEM((chips, size, k), F32), pltpu.SemaphoreType.DMA((chips,))],
            aliases={chips: 0} if extra else None,
            out_specs=[hbm],
        )[0]
    return (embedding, centroids)


def solution(mesh):
    placed = (
        P("blk", None),
        P(("blk", "col"), None),
        P(("blk", "col"), None),
        P(("blk", "col")),
        P(),
        P("blk", None),
        P(("blk", "col")),
    )

    return jax.shard_map(body, mesh=mesh, in_specs=placed, out_specs=(P(("blk", "col"), None), P()), check_vma=False)
```

```python
import functools
import math

import jax
import jax.numpy as jnp
from jax import lax
from jax.experimental import pallas as pl
from jax.experimental.pallas import tpu as pltpu
from jax.sharding import PartitionSpec as P


C = 1000
BLOCK = 128
TAIL = 8
HEAVY = 5_000_000_000
DEAD = 1e30
LOG2E = 1.4426950408889634
F32 = jnp.float32
BF16 = jnp.bfloat16


VMEM = pl.BlockSpec(memory_space=pltpu.VMEM)


def call(kernel, outs, args, specs=None, scratch=(), flops=1000, mib=16, aliases=None, out_specs=None):
    nbytes = sum(a.size * a.dtype.itemsize for a in list(args) + list(outs))
    return pl.pallas_call(
        kernel,
        out_shape=outs,
        in_specs=specs or [VMEM] * len(args),
        out_specs=out_specs or [VMEM] * len(outs),
        scratch_shapes=list(scratch),
        input_output_aliases=aliases or {},
        compiler_params=pltpu.CompilerParams(vmem_limit_bytes=mib << 20),
        cost_estimate=pl.CostEstimate(flops=flops, bytes_accessed=nbytes, transcendentals=0),
    )(*args)


def struct(shape, dtype):
    return jax.ShapeDtypeStruct(shape, dtype)


def eye(rows, cols):
    return lax.broadcasted_iota(jnp.int32, (rows, cols), 0) == lax.broadcasted_iota(
        jnp.int32, (rows, cols), 1
    )


def to_row(col, cols):
    n = col.shape[0]
    return jnp.sum(jnp.where(eye(n, cols), jnp.broadcast_to(col, (n, cols)), 0.0), 0, keepdims=True)


def to_col(row, rows):
    n = row.shape[1]
    return jnp.sum(jnp.where(eye(rows, n), jnp.broadcast_to(row, (rows, n)), 0.0), 1, keepdims=True)


def spot_kernel(out_ref):
    out_ref[...] = lax.broadcasted_iota(jnp.int32, out_ref.shape, 1)


def prep_kernel(spot_ref, land_ref, vec_ref, deg_ref, val_ref, out_ref, *halves):
    features = land_ref.shape[1]
    rows = land_ref.shape[0]
    for start in range(0, features, rows):
        part = land_ref[:, start : start + rows]
        out_ref[:, start : start + rows] = part.T
    here = lax.broadcasted_iota(jnp.int32, (rows, rows), 0) == spot_ref[:1, :]
    root = jnp.sum(
        jnp.where(here, jnp.broadcast_to(lax.rsqrt(deg_ref[...]), (rows, rows)), 0.0), 1, keepdims=True
    )
    out_ref[:, features:] = (vec_ref[...].astype(F32) * root / val_ref[...]).astype(BF16)
    for n, half in enumerate(halves):
        width = half.shape[1]
        half[...] = out_ref[:, n * width : (n + 1) * width]


def take(piece, start, size):
    width = piece[0].shape[1]
    return piece[start // width][:, start % width : start % width + size]


def owner_of(place):
    me = lax.axis_index("blk")
    even, odd = place
    return jnp.bitwise_xor(me, even if even == odd else jnp.where(me % 2 == 0, even, odd))


def weigh(places, k, doc_ref, square_ref, mask_ref, pieces, low_ref, window, add_degree, add_total):
    base, count, step = window
    features = doc_ref.shape[1]
    land_rows = pieces[0][0].shape[0]
    width = len(pieces) * land_rows
    scale = 4.0 / features * LOG2E
    col = lax.axis_index("col")
    cols = lax.axis_size("col")
    lands = jnp.concatenate(
        [
            jnp.concatenate([take(p, start, land_rows) for p in pieces], 1)
            for start in range(0, features, land_rows)
        ],
        0,
    )
    vectors = jnp.concatenate([take(p, features, k) for p in pieces], 0)
    wide = lands.astype(F32)
    land_square = scale * jnp.sum(wide * wide, 0, keepdims=True)
    live = mask_ref[...].astype(F32)
    lane = lax.broadcasted_iota(jnp.int32, live.shape, 1)
    line = lax.broadcasted_iota(jnp.int32, (live.shape[0], 1), 0)
    flags = [
        jnp.sum(jnp.where(lane == owner_of(place) * cols + col, live, 0.0), 1, keepdims=True)
        for place in places
    ]
    whole = pl.ds(base, count)
    prod = jnp.dot(doc_ref[whole, :], lands, preferred_element_type=F32)
    for start in range(0, count, step):
        rows, local = pl.ds(base + start, step), slice(start, start + step)
        block = (base + start) // BLOCK
        less = jnp.concatenate(
            [
                jnp.where(
                    jnp.sum(jnp.where(line == block, flag, 0.0), 0, keepdims=True) > 0.0,
                    land_square[:, n * land_rows : (n + 1) * land_rows],
                    DEAD,
                )
                for n, flag in enumerate(flags)
            ],
            1,
        )
        weights = jnp.exp2((2.0 * scale) * prod[local] - square_ref[rows, :][:, :1] - less)
        low_ref[local, :width] = weights.astype(BF16)
        part = weights[:, :128]
        for j in range(1, width // 128):
            part = part + weights[:, j * 128 : (j + 1) * 128]
        add_degree(rows, local, part)
    add_total(whole, jnp.dot(low_ref[:count, :width], vectors, preferred_element_type=F32))


def split_parts(places, refs):
    pieces = []
    for count, _ in places:
        pieces.append(refs[:count])
        refs = refs[count:]
    return pieces, refs


def first_kernel(places, doc_ref, mask_ref, *refs):
    pieces, (total_ref, degree_ref, square_ref, low_ref) = split_parts(places, refs)
    total_k = total_ref.shape[1]
    scale = 4.0 / doc_ref.shape[1] * LOG2E
    for i in range(doc_ref.shape[0] // BLOCK):
        rows = pl.ds(i * BLOCK, BLOCK)
        block = doc_ref[rows, :].astype(F32)
        total = scale * jnp.sum(block * block, 1, keepdims=True)
        square_ref[rows, :] = jnp.broadcast_to(total, (BLOCK, 128))

    def add_degree(rows, local, part):
        degree_ref[rows, :] = part

    def add_total(rows, part):
        total_ref[rows, :] = part

    window = 0, doc_ref.shape[0], BLOCK
    weigh([place for _, place in places], total_k, doc_ref, square_ref, mask_ref, pieces, low_ref, window, add_degree, add_total)


def more_kernel(places, doc_ref, square_ref, mask_ref, total_in, degree_in, *refs):
    pieces, (total_ref, degree_ref, low_ref) = split_parts(places, refs)
    total_k = total_ref.shape[1]

    def add_degree(rows, local, part):
        degree_ref[rows, :] = degree_in[rows, :] + part

    def add_total(rows, part):
        total_ref[rows, :] = total_in[rows, :] + part

    window = 0, doc_ref.shape[0], BLOCK
    weigh([place for _, place in places], total_k, doc_ref, square_ref, mask_ref, pieces, low_ref, window, add_degree, add_total)


def part_kernel(mask, places, doc_ref, square_ref, mask_ref, total_in, degree_in, *refs):
    pieces, refs = split_parts(places, refs)
    outs, (low_ref, part_ref) = refs[:-2], refs[-2:]
    n, k = low_ref.shape[0], total_in.shape[1]
    total_k = k
    step = math.gcd(n, BLOCK)
    base = pl.multiple_of(jnp.bitwise_xor(lax.axis_index("col"), mask) * n, step)
    totals = []

    def add_degree(rows, local, part):
        part_ref[local, :] = degree_in[rows, :] + part

    def add_total(rows, part):
        totals.append(total_in[rows, :] + part)

    window = base, n, step
    weigh([place for _, place in places], total_k, doc_ref, square_ref, mask_ref, pieces, low_ref, window, add_degree, add_total)
    deg = to_row(jnp.sum(part_ref[...], 1, keepdims=True), k)
    if mask == 0:
        outs[0][...] = totals[0]
        outs[1][...] = jnp.broadcast_to(deg, outs[1].shape)
    else:
        outs[0][:n, :] = totals[0].astype(BF16)
        high = deg.astype(BF16).astype(F32)
        spot = lax.broadcasted_iota(jnp.int32, (TAIL, k), 0)
        tail = jnp.where(spot == 0, high, jnp.where(spot == 1, deg - high, 0.0))
        outs[0][n:, :] = tail.astype(BF16)


def embed(own_ref, own_deg_ref, gets):
    n = own_ref.shape[0]
    proj = own_ref[...]
    deg = own_deg_ref[:1, :]
    for get in gets:
        proj = proj + get[:n, :].astype(F32)
        tail = get[n:, :].astype(F32)
        deg = deg + (tail[:1, :] + tail[1:2, :])
    return proj * lax.rsqrt(to_col(deg, n))


def embed_kernel(own_ref, own_deg_ref, *refs):
    refs[-1][...] = embed(own_ref, own_deg_ref, refs[:-1])


def gather_rows(core, label_ref, high, low, out_ref):
    me = lax.axis_index("blk")
    chips = lax.axis_size("blk") // 2
    n = high.shape[0]
    size = out_ref.shape[0] // chips
    labels = jnp.broadcast_to(label_ref[...], (size, n))
    spot = lax.broadcasted_iota(jnp.int32, (size, n), 0)
    for chip in range(chips):
        owner = jnp.bitwise_xor(me, 2 * chip + core)
        hot = jnp.where(labels == spot + owner * size, 1.0, 0.0).astype(BF16)
        part = jnp.dot(hot, high, preferred_element_type=F32)
        part = part + jnp.dot(hot, low, preferred_element_type=F32)
        out_ref[chip * size : (chip + 1) * size, :] = part.astype(out_ref.dtype)


def norm_kernel(own_ref, own_deg_ref, label_ref, *refs):
    send_ref, high_ref, low_ref = refs[-3:]
    emb = embed(own_ref, own_deg_ref, refs[:-3])
    unit = emb * lax.rsqrt(jnp.sum(emb * emb, 1, keepdims=True) + 1e-06)
    high = unit.astype(BF16)
    low = (unit - high.astype(F32)).astype(BF16)
    high_ref[...] = high
    low_ref[...] = low
    gather_rows(1, label_ref, high, low, send_ref)


def keep_kernel(label_ref, high_ref, low_ref, keep_ref):
    gather_rows(0, label_ref, high_ref[...], low_ref[...], keep_ref)


def split_kernel(keep_ref, get_ref, own_ref, *sends):
    size = own_ref.shape[0]
    for chip in range(len(sends) + 1):
        rows = slice(chip * size, (chip + 1) * size)
        both = keep_ref[rows, :] + get_ref[rows, :].astype(F32)
        out = sends[chip - 1] if chip else own_ref
        out[...] = both.astype(out.dtype)


def tree(parts):
    while len(parts) > 1:
        parts = [a + b for a, b in zip(parts[::2], parts[1::2])]
    return parts[0]


def sum_kernel(*refs):
    refs[-1][...] = tree([ref[...].astype(F32) for ref in refs[:-1]]).astype(refs[-1].dtype)


def place_kernel(places, aliased, *refs):
    parts, (out_hbm, wide_ref, sem) = refs[: len(places)], refs[-3:]
    del aliased
    size = parts[0].shape[0]
    count = out_hbm.shape[0]
    whole, rest = count // size, count % size
    copies = []
    for n, (place, part) in enumerate(zip(places, parts)):
        owner = jnp.bitwise_xor(lax.axis_index("blk"), place)
        wide_ref[n] = part[...].astype(F32)
        full = pltpu.make_async_copy(
            wide_ref.at[n],
            out_hbm.at[pl.ds(pl.multiple_of(jnp.minimum(owner, whole - 1) * size, 8), size), :],
            sem.at[n],
        )
        copies.append((owner < whole, full))
        if rest:
            end = pltpu.make_async_copy(
                wide_ref.at[n, pl.ds(0, rest), :], out_hbm.at[pl.ds(whole * size, rest), :], sem.at[n]
            )
            copies.append((owner == whole, end))
    for here, copy in copies:
        pl.when(here)(copy.start)
    for here, copy in copies:
        pl.when(here)(copy.wait)


def body(documents, landmarks, eigen_vectors, land_degree, eigen_values, tile_mask, labels):
    blks, cols = lax.axis_size("blk"), lax.axis_size("col")
    chips = blks // 2
    doc_rows, features = documents.shape
    land_rows = landmarks.shape[0]
    k = eigen_vectors.shape[1]
    rows = doc_rows // cols
    assert rows <= k and doc_rows % BLOCK == 0 and land_rows == BLOCK and features % BLOCK == 0

    def swap(x, pick):
        return lax.ppermute(x, "blk", [(i, pick(i)) for i in range(blks)])

    def core_swap(x):
        return swap(x, lambda i: i ^ 1)

    def chip_swap(x, mask):
        return swap(x, lambda i: i ^ (2 * mask))

    def col_swap(x, mask):
        return lax.ppermute(x, "col", [(i, i ^ mask) for i in range(cols)])

    spot = call(spot_kernel, [struct((8, land_rows), jnp.int32)], [], flops=HEAVY)[0]
    width = features + k
    split_a = chips == 4 and width % (2 * land_rows) == 0 and features * 2 >= width
    half = [struct((land_rows, width // 2), BF16)] * 2 if split_a else []
    own, *halves = call(
        prep_kernel,
        [struct((land_rows, width), BF16)] + half,
        [spot, landmarks, eigen_vectors, land_degree.reshape(1, -1), eigen_values.reshape(1, -1)],
        flops=HEAVY,
    )

    if chips == 4:
        step_a = lambda i: i ^ 2 if i % 2 == 0 else i ^ 4
        step_b = lambda i: i ^ 4 if i % 2 == 0 else i ^ 2
        got_a = [swap(x, step_a) for x in halves or [own]]
        got_b = swap(own, step_b)
        got_f = [swap(x, step_b) for x in got_a]
        far_own, far_b = core_swap(own), core_swap(got_b)
        far_a = [core_swap(x) for x in got_a]
        far_f = [core_swap(x) for x in got_f]
        groups = [
            [([own], (0, 0)), ([far_own], (1, 1))],
            [(got_a, (2, 4)), (far_a, (5, 3))],
            [([got_b], (4, 2)), ([far_b], (3, 5))],
            [(got_f, (6, 6)), (far_f, (7, 7))],
        ]
    else:
        near = [own] + [chip_swap(own, mask) for mask in range(1, chips)]
        groups = [
            [([x], (2 * mask, 2 * mask)), ([core_swap(x)], (2 * mask + 1, 2 * mask + 1))]
            for mask, x in enumerate(near)
        ]

    scratch = [pltpu.VMEM((doc_rows, 2 * land_rows), BF16)]
    sums = [struct((doc_rows, k), F32), struct((doc_rows, 128), F32)]

    def run(kernel, group, outs, args, scratch, aliases=None, share=1):
        places = [(len(parts), place) for parts, place in group]
        args = args + [part for parts, _ in group for part in parts]
        flops = len(group) * 2 * doc_rows * land_rows * (features + k) // share
        kernel = functools.partial(kernel, places)
        return call(kernel, outs, args, None, scratch, flops, aliases=aliases)

    *state, square = run(first_kernel, groups[0], sums + sums[1:], [documents, tile_mask], scratch)
    head = [documents, square, tile_mask]
    for group in groups[1:-1]:
        state = run(more_kernel, group, sums, head + list(state), scratch, {3: 0, 4: 1})
    narrow = [pltpu.VMEM((rows, len(groups[-1]) * land_rows), BF16), pltpu.VMEM((rows, 128), F32)]

    def part(mask, outs):
        kernel = functools.partial(part_kernel, mask)
        return run(kernel, groups[-1], outs, head + list(state), narrow, share=cols)

    parts = part(0, [struct((rows, k), F32), struct((8, k), F32)])
    sends = [part(mask, [struct((rows + TAIL, k), BF16)])[0] for mask in range(1, cols)]
    gets = [col_swap(x, mask + 1) for mask, x in enumerate(sends)]
    size = -(-(-(-C // blks)) // 16) * 16
    names = labels.reshape(1, -1)
    wide, half = struct((chips * size, k), F32), struct((chips * size, k), BF16)
    unit = struct((rows, k), BF16)
    send, high, low = call(norm_kernel, [half, unit, unit], [parts[0], parts[1], names, *gets])
    get = core_swap(send)
    keep = call(keep_kernel, [wide], [names, high, low])[0]
    embedding = call(embed_kernel, [struct((rows, k), F32)], [parts[0], parts[1], *gets])[0]
    one, low = struct((size, k), F32), struct((size, k), BF16)
    split = call(split_kernel, [one] + [low] * (chips - 1), [keep, get])
    gets = [chip_swap(x, mask + 1) for mask, x in enumerate(split[1:])]
    mine = call(sum_kernel, [low], [split[0], *gets])[0]
    gets = [col_swap(mine, mask) for mask in range(1, cols)]
    done = call(sum_kernel, [low], [mine, *gets])[0]
    near = [done] + [chip_swap(done, mask) for mask in range(1, chips)]
    far = [core_swap(x) for x in near]
    centroids = None
    hbm = pl.BlockSpec(memory_space=pl.ANY)
    for core, chunks in enumerate((near, far)):
        extra = [] if centroids is None else [centroids]
        centroids = call(
            functools.partial(place_kernel, [2 * mask + core for mask in range(chips)], bool(extra)),
            [struct((C, k), F32)],
            chunks + extra,
            [VMEM] * chips + [hbm] * len(extra),
            [pltpu.VMEM((chips, size, k), F32), pltpu.SemaphoreType.DMA((chips,))],
            aliases={chips: 0} if extra else None,
            out_specs=[hbm],
        )[0]
    return (embedding, centroids)


def solution(mesh):
    placed = (
        P("blk", None),
        P(("blk", "col"), None),
        P(("blk", "col"), None),
        P(("blk", "col")),
        P(),
        P("blk", None),
        P(("blk", "col")),
    )

    return jax.shard_map(body, mesh=mesh, in_specs=placed, out_specs=(P(("blk", "col"), None), P()), check_vma=False)
```

```python
import functools
import math

import jax
import jax.numpy as jnp
from jax import lax
from jax.experimental import pallas as pl
from jax.experimental.pallas import tpu as pltpu
from jax.sharding import PartitionSpec as P


C = 1000
BLOCK = 128
TAIL = 8
HEAVY = 5_000_000_000
DEAD = 1e30
LOG2E = 1.4426950408889634
F32 = jnp.float32
BF16 = jnp.bfloat16


VMEM = pl.BlockSpec(memory_space=pltpu.VMEM)


def call(kernel, outs, args, specs=None, scratch=(), flops=1000, mib=16, aliases=None, out_specs=None):
    nbytes = sum(a.size * a.dtype.itemsize for a in list(args) + list(outs))
    return pl.pallas_call(
        kernel,
        out_shape=outs,
        in_specs=specs or [VMEM] * len(args),
        out_specs=out_specs or [VMEM] * len(outs),
        scratch_shapes=list(scratch),
        input_output_aliases=aliases or {},
        compiler_params=pltpu.CompilerParams(vmem_limit_bytes=mib << 20),
        cost_estimate=pl.CostEstimate(flops=flops, bytes_accessed=nbytes, transcendentals=0),
    )(*args)


def struct(shape, dtype):
    return jax.ShapeDtypeStruct(shape, dtype)


def eye(rows, cols):
    return lax.broadcasted_iota(jnp.int32, (rows, cols), 0) == lax.broadcasted_iota(
        jnp.int32, (rows, cols), 1
    )


def to_row(col, cols):
    n = col.shape[0]
    return jnp.sum(jnp.where(eye(n, cols), jnp.broadcast_to(col, (n, cols)), 0.0), 0, keepdims=True)


def to_col(row, rows):
    n = row.shape[1]
    return jnp.sum(jnp.where(eye(rows, n), jnp.broadcast_to(row, (rows, n)), 0.0), 1, keepdims=True)


def spot_kernel(out_ref):
    out_ref[...] = lax.broadcasted_iota(jnp.int32, out_ref.shape, 1)


def prep_kernel(spot_ref, land_ref, vec_ref, deg_ref, val_ref, out_ref, *halves):
    features = land_ref.shape[1]
    rows = land_ref.shape[0]
    for start in range(0, features, rows):
        part = land_ref[:, start : start + rows]
        out_ref[:, start : start + rows] = part.T
    here = lax.broadcasted_iota(jnp.int32, (rows, rows), 0) == spot_ref[:1, :]
    root = jnp.sum(
        jnp.where(here, jnp.broadcast_to(lax.rsqrt(deg_ref[...]), (rows, rows)), 0.0), 1, keepdims=True
    )
    out_ref[:, features:] = (vec_ref[...].astype(F32) * root / val_ref[...]).astype(BF16)
    for n, half in enumerate(halves):
        width = half.shape[1]
        half[...] = out_ref[:, n * width : (n + 1) * width]


def take(piece, start, size):
    width = piece[0].shape[1]
    return piece[start // width][:, start % width : start % width + size]


def owner_of(place):
    me = lax.axis_index("blk")
    even, odd = place
    return jnp.bitwise_xor(me, even if even == odd else jnp.where(me % 2 == 0, even, odd))


def weigh(places, k, doc_ref, square_ref, mask_ref, pieces, low_ref, window, add_degree, add_total):
    base, count, step = window
    features = doc_ref.shape[1]
    land_rows = pieces[0][0].shape[0]
    width = len(pieces) * land_rows
    scale = 4.0 / features * LOG2E
    col = lax.axis_index("col")
    cols = lax.axis_size("col")
    lands = jnp.concatenate(
        [
            jnp.concatenate([take(p, start, land_rows) for p in pieces], 1)
            for start in range(0, features, land_rows)
        ],
        0,
    )
    vectors = jnp.concatenate([take(p, features, k) for p in pieces], 0)
    wide = lands.astype(F32)
    land_square = scale * jnp.sum(wide * wide, 0, keepdims=True)
    live = mask_ref[...].astype(F32)
    lane = lax.broadcasted_iota(jnp.int32, live.shape, 1)
    line = lax.broadcasted_iota(jnp.int32, (live.shape[0], 1), 0)
    flags = [
        jnp.sum(jnp.where(lane == owner_of(place) * cols + col, live, 0.0), 1, keepdims=True)
        for place in places
    ]
    whole = pl.ds(base, count)
    prod = jnp.dot(doc_ref[whole, :], lands, preferred_element_type=F32)
    for start in range(0, count, step):
        rows, local = pl.ds(base + start, step), slice(start, start + step)
        block = (base + start) // BLOCK
        less = jnp.concatenate(
            [
                jnp.where(
                    jnp.sum(jnp.where(line == block, flag, 0.0), 0, keepdims=True) > 0.0,
                    land_square[:, n * land_rows : (n + 1) * land_rows],
                    DEAD,
                )
                for n, flag in enumerate(flags)
            ],
            1,
        )
        weights = jnp.exp2((2.0 * scale) * prod[local] - square_ref[rows, :][:, :1] - less)
        low_ref[local, :width] = weights.astype(BF16)
        part = weights[:, :128]
        for j in range(1, width // 128):
            part = part + weights[:, j * 128 : (j + 1) * 128]
        add_degree(rows, local, part)
    add_total(whole, jnp.dot(low_ref[:count, :width], vectors, preferred_element_type=F32))


def split_parts(places, refs):
    pieces = []
    for count, _ in places:
        pieces.append(refs[:count])
        refs = refs[count:]
    return pieces, refs


def first_kernel(places, doc_ref, mask_ref, *refs):
    pieces, (total_ref, degree_ref, square_ref, low_ref) = split_parts(places, refs)
    total_k = total_ref.shape[1]
    scale = 4.0 / doc_ref.shape[1] * LOG2E
    for i in range(doc_ref.shape[0] // BLOCK):
        rows = pl.ds(i * BLOCK, BLOCK)
        block = doc_ref[rows, :].astype(F32)
        total = scale * jnp.sum(block * block, 1, keepdims=True)
        square_ref[rows, :] = jnp.broadcast_to(total, (BLOCK, 128))

    def add_degree(rows, local, part):
        degree_ref[rows, :] = part

    def add_total(rows, part):
        total_ref[rows, :] = part

    window = 0, doc_ref.shape[0], BLOCK
    weigh([place for _, place in places], total_k, doc_ref, square_ref, mask_ref, pieces, low_ref, window, add_degree, add_total)


def more_kernel(places, doc_ref, square_ref, mask_ref, total_in, degree_in, *refs):
    pieces, (total_ref, degree_ref, low_ref) = split_parts(places, refs)
    total_k = total_ref.shape[1]

    def add_degree(rows, local, part):
        degree_ref[rows, :] = degree_in[rows, :] + part

    def add_total(rows, part):
        total_ref[rows, :] = total_in[rows, :] + part

    window = 0, doc_ref.shape[0], BLOCK
    weigh([place for _, place in places], total_k, doc_ref, square_ref, mask_ref, pieces, low_ref, window, add_degree, add_total)


def part_kernel(mask, places, doc_ref, square_ref, mask_ref, total_in, degree_in, *refs):
    pieces, refs = split_parts(places, refs)
    outs, (low_ref, part_ref) = refs[:-2], refs[-2:]
    n, k = low_ref.shape[0], total_in.shape[1]
    total_k = k
    step = math.gcd(n, BLOCK)
    base = pl.multiple_of(jnp.bitwise_xor(lax.axis_index("col"), mask) * n, step)
    totals = []

    def add_degree(rows, local, part):
        part_ref[local, :] = degree_in[rows, :] + part

    def add_total(rows, part):
        totals.append(total_in[rows, :] + part)

    window = base, n, step
    weigh([place for _, place in places], total_k, doc_ref, square_ref, mask_ref, pieces, low_ref, window, add_degree, add_total)
    deg = to_row(jnp.sum(part_ref[...], 1, keepdims=True), k)
    if mask == 0:
        outs[0][...] = totals[0]
        outs[1][...] = jnp.broadcast_to(deg, outs[1].shape)
    else:
        outs[0][:n, :] = totals[0].astype(BF16)
        high = deg.astype(BF16).astype(F32)
        spot = lax.broadcasted_iota(jnp.int32, (TAIL, k), 0)
        tail = jnp.where(spot == 0, high, jnp.where(spot == 1, deg - high, 0.0))
        outs[0][n:, :] = tail.astype(BF16)


def embed(own_ref, own_deg_ref, gets):
    n = own_ref.shape[0]
    proj = own_ref[...]
    deg = own_deg_ref[:1, :]
    for get in gets:
        proj = proj + get[:n, :].astype(F32)
        tail = get[n:, :].astype(F32)
        deg = deg + (tail[:1, :] + tail[1:2, :])
    return proj * lax.rsqrt(to_col(deg, n))


def embed_kernel(own_ref, own_deg_ref, *refs):
    refs[-1][...] = embed(own_ref, own_deg_ref, refs[:-1])


def gather_rows(core, label_ref, high, low, out_ref):
    me = lax.axis_index("blk")
    chips = lax.axis_size("blk") // 2
    n = high.shape[0]
    size = out_ref.shape[0] // chips
    labels = jnp.broadcast_to(label_ref[...], (size, n))
    spot = lax.broadcasted_iota(jnp.int32, (size, n), 0)
    for chip in range(chips):
        owner = jnp.bitwise_xor(me, 2 * chip + core)
        hot = jnp.where(labels == spot + owner * size, 1.0, 0.0).astype(BF16)
        part = jnp.dot(hot, high, preferred_element_type=F32)
        part = part + jnp.dot(hot, low, preferred_element_type=F32)
        out_ref[chip * size : (chip + 1) * size, :] = part.astype(out_ref.dtype)


def norm_kernel(own_ref, own_deg_ref, label_ref, *refs):
    send_ref, high_ref, low_ref = refs[-3:]
    emb = embed(own_ref, own_deg_ref, refs[:-3])
    unit = emb * lax.rsqrt(jnp.sum(emb * emb, 1, keepdims=True) + 1e-06)
    high = unit.astype(BF16)
    low = (unit - high.astype(F32)).astype(BF16)
    high_ref[...] = high
    low_ref[...] = low
    gather_rows(1, label_ref, high, low, send_ref)


def keep_kernel(label_ref, high_ref, low_ref, keep_ref):
    gather_rows(0, label_ref, high_ref[...], low_ref[...], keep_ref)


def split_kernel(keep_ref, get_ref, own_ref, *sends):
    size = own_ref.shape[0]
    for chip in range(len(sends) + 1):
        rows = slice(chip * size, (chip + 1) * size)
        both = keep_ref[rows, :] + get_ref[rows, :].astype(F32)
        out = sends[chip - 1] if chip else own_ref
        out[...] = both.astype(out.dtype)


def tree(parts):
    while len(parts) > 1:
        parts = [a + b for a, b in zip(parts[::2], parts[1::2])]
    return parts[0]


def sum_kernel(*refs):
    refs[-1][...] = tree([ref[...].astype(F32) for ref in refs[:-1]]).astype(refs[-1].dtype)


def place_kernel(places, aliased, *refs):
    parts, (out_hbm, wide_ref, sem) = refs[: len(places)], refs[-3:]
    del aliased
    size = parts[0].shape[0]
    count = out_hbm.shape[0]
    whole, rest = count // size, count % size
    copies = []
    for n, (place, part) in enumerate(zip(places, parts)):
        owner = jnp.bitwise_xor(lax.axis_index("blk"), place)
        wide_ref[n] = part[...].astype(F32)
        full = pltpu.make_async_copy(
            wide_ref.at[n],
            out_hbm.at[pl.ds(pl.multiple_of(jnp.minimum(owner, whole - 1) * size, 8), size), :],
            sem.at[n],
        )
        here = [(owner < whole, full)]
        if rest:
            end = pltpu.make_async_copy(
                wide_ref.at[n, pl.ds(0, rest), :], out_hbm.at[pl.ds(whole * size, rest), :], sem.at[n]
            )
            here.append((owner == whole, end))
        for flag, copy in here:
            pl.when(flag)(copy.start)
        copies += here
    for flag, copy in copies:
        pl.when(flag)(copy.wait)


def body(documents, landmarks, eigen_vectors, land_degree, eigen_values, tile_mask, labels):
    blks, cols = lax.axis_size("blk"), lax.axis_size("col")
    chips = blks // 2
    doc_rows, features = documents.shape
    land_rows = landmarks.shape[0]
    k = eigen_vectors.shape[1]
    rows = doc_rows // cols
    assert rows <= k and doc_rows % BLOCK == 0 and land_rows == BLOCK and features % BLOCK == 0

    def swap(x, pick):
        return lax.ppermute(x, "blk", [(i, pick(i)) for i in range(blks)])

    def core_swap(x):
        return swap(x, lambda i: i ^ 1)

    def chip_swap(x, mask):
        return swap(x, lambda i: i ^ (2 * mask))

    def col_swap(x, mask):
        return lax.ppermute(x, "col", [(i, i ^ mask) for i in range(cols)])

    spot = call(spot_kernel, [struct((8, land_rows), jnp.int32)], [], flops=HEAVY)[0]
    width = features + k
    split_a = chips == 4 and width % (2 * land_rows) == 0 and features * 2 >= width
    half = [struct((land_rows, width // 2), BF16)] * 2 if split_a else []
    own, *halves = call(
        prep_kernel,
        [struct((land_rows, width), BF16)] + half,
        [spot, landmarks, eigen_vectors, land_degree.reshape(1, -1), eigen_values.reshape(1, -1)],
        flops=HEAVY,
    )

    if chips == 4:
        step_a = lambda i: i ^ 2 if i % 2 == 0 else i ^ 4
        step_b = lambda i: i ^ 4 if i % 2 == 0 else i ^ 2
        got_a = [swap(x, step_a) for x in halves or [own]]
        got_b = swap(own, step_b)
        got_f = [swap(x, step_b) for x in got_a]
        far_own, far_b = core_swap(own), core_swap(got_b)
        far_a = [core_swap(x) for x in got_a]
        far_f = [core_swap(x) for x in got_f]
        groups = [
            [([own], (0, 0)), ([far_own], (1, 1))],
            [(got_a, (2, 4)), (far_a, (5, 3))],
            [([got_b], (4, 2)), ([far_b], (3, 5))],
            [(got_f, (6, 6)), (far_f, (7, 7))],
        ]
    else:
        near = [own] + [chip_swap(own, mask) for mask in range(1, chips)]
        groups = [
            [([x], (2 * mask, 2 * mask)), ([core_swap(x)], (2 * mask + 1, 2 * mask + 1))]
            for mask, x in enumerate(near)
        ]

    scratch = [pltpu.VMEM((doc_rows, 2 * land_rows), BF16)]
    sums = [struct((doc_rows, k), F32), struct((doc_rows, 128), F32)]

    def run(kernel, group, outs, args, scratch, aliases=None, share=1):
        places = [(len(parts), place) for parts, place in group]
        args = args + [part for parts, _ in group for part in parts]
        flops = len(group) * 2 * doc_rows * land_rows * (features + k) // share
        kernel = functools.partial(kernel, places)
        return call(kernel, outs, args, None, scratch, flops, aliases=aliases)

    *state, square = run(first_kernel, groups[0], sums + sums[1:], [documents, tile_mask], scratch)
    head = [documents, square, tile_mask]
    for group in groups[1:-1]:
        state = run(more_kernel, group, sums, head + list(state), scratch, {3: 0, 4: 1})
    narrow = [pltpu.VMEM((rows, len(groups[-1]) * land_rows), BF16), pltpu.VMEM((rows, 128), F32)]

    def part(mask, outs):
        kernel = functools.partial(part_kernel, mask)
        return run(kernel, groups[-1], outs, head + list(state), narrow, share=cols)

    parts = part(0, [struct((rows, k), F32), struct((8, k), F32)])
    sends = [part(mask, [struct((rows + TAIL, k), BF16)])[0] for mask in range(1, cols)]
    gets = [col_swap(x, mask + 1) for mask, x in enumerate(sends)]
    size = -(-(-(-C // blks)) // 16) * 16
    names = labels.reshape(1, -1)
    wide, half = struct((chips * size, k), F32), struct((chips * size, k), BF16)
    unit = struct((rows, k), BF16)
    send, high, low = call(norm_kernel, [half, unit, unit], [parts[0], parts[1], names, *gets])
    get = core_swap(send)
    keep = call(keep_kernel, [wide], [names, high, low])[0]
    embedding = call(embed_kernel, [struct((rows, k), F32)], [parts[0], parts[1], *gets])[0]
    one, low = struct((size, k), F32), struct((size, k), BF16)
    split = call(split_kernel, [one] + [low] * (chips - 1), [keep, get])
    gets = [chip_swap(x, mask + 1) for mask, x in enumerate(split[1:])]
    mine = call(sum_kernel, [low], [split[0], *gets])[0]
    gets = [col_swap(mine, mask) for mask in range(1, cols)]
    done = call(sum_kernel, [low], [mine, *gets])[0]
    near = [done] + [chip_swap(done, mask) for mask in range(1, chips)]
    far = [core_swap(x) for x in near]
    centroids = None
    hbm = pl.BlockSpec(memory_space=pl.ANY)
    chunks = [(x, 2 * mask) for mask, x in enumerate(near)] + [(x, 2 * mask + 1) for mask, x in enumerate(far)]
    for some in (chunks[: chips + 1], chunks[chips + 1 :]):
        extra = [] if centroids is None else [centroids]
        centroids = call(
            functools.partial(place_kernel, [place for _, place in some], bool(extra)),
            [struct((C, k), F32)],
            [x for x, _ in some] + extra,
            [VMEM] * len(some) + [hbm] * len(extra),
            [pltpu.VMEM((len(some), size, k), F32), pltpu.SemaphoreType.DMA((len(some),))],
            aliases={len(some): 0} if extra else None,
            out_specs=[hbm],
        )[0]
    return (embedding, centroids)


def solution(mesh):
    placed = (
        P("blk", None),
        P(("blk", "col"), None),
        P(("blk", "col"), None),
        P(("blk", "col")),
        P(),
        P("blk", None),
        P(("blk", "col")),
    )

    return jax.shard_map(body, mesh=mesh, in_specs=placed, out_specs=(P(("blk", "col"), None), P()), check_vma=False)
```

```python
import functools
import math

import jax
import jax.numpy as jnp
from jax import lax
from jax.experimental import pallas as pl
from jax.experimental.pallas import tpu as pltpu
from jax.sharding import PartitionSpec as P


C = 1000
BLOCK = 128
TAIL = 8
HEAVY = 5_000_000_000
DEAD = 1e30
LOG2E = 1.4426950408889634
F32 = jnp.float32
BF16 = jnp.bfloat16


VMEM = pl.BlockSpec(memory_space=pltpu.VMEM)


def call(kernel, outs, args, specs=None, scratch=(), flops=1000, mib=16, aliases=None, out_specs=None):
    nbytes = sum(a.size * a.dtype.itemsize for a in list(args) + list(outs))
    return pl.pallas_call(
        kernel,
        out_shape=outs,
        in_specs=specs or [VMEM] * len(args),
        out_specs=out_specs or [VMEM] * len(outs),
        scratch_shapes=list(scratch),
        input_output_aliases=aliases or {},
        compiler_params=pltpu.CompilerParams(vmem_limit_bytes=mib << 20),
        cost_estimate=pl.CostEstimate(flops=flops, bytes_accessed=nbytes, transcendentals=0),
    )(*args)


def struct(shape, dtype):
    return jax.ShapeDtypeStruct(shape, dtype)


def eye(rows, cols):
    return lax.broadcasted_iota(jnp.int32, (rows, cols), 0) == lax.broadcasted_iota(
        jnp.int32, (rows, cols), 1
    )


def to_row(col, cols):
    n = col.shape[0]
    return jnp.sum(jnp.where(eye(n, cols), jnp.broadcast_to(col, (n, cols)), 0.0), 0, keepdims=True)


def to_col(row, rows):
    n = row.shape[1]
    return jnp.sum(jnp.where(eye(rows, n), jnp.broadcast_to(row, (rows, n)), 0.0), 1, keepdims=True)


def spot_kernel(out_ref):
    out_ref[...] = lax.broadcasted_iota(jnp.int32, out_ref.shape, 1)


def prep_kernel(spot_ref, land_ref, vec_ref, deg_ref, val_ref, out_ref, *halves):
    features = land_ref.shape[1]
    rows = land_ref.shape[0]
    for start in range(0, features, rows):
        part = land_ref[:, start : start + rows]
        out_ref[:, start : start + rows] = part.T
    here = lax.broadcasted_iota(jnp.int32, (rows, rows), 0) == spot_ref[:1, :]
    root = jnp.sum(
        jnp.where(here, jnp.broadcast_to(lax.rsqrt(deg_ref[...]), (rows, rows)), 0.0), 1, keepdims=True
    )
    out_ref[:, features:] = (vec_ref[...].astype(F32) * root / val_ref[...]).astype(BF16)
    for n, half in enumerate(halves):
        width = half.shape[1]
        half[...] = out_ref[:, n * width : (n + 1) * width]


def take(piece, start, size):
    width = piece[0].shape[1]
    return piece[start // width][:, start % width : start % width + size]


def owner_of(place):
    me = lax.axis_index("blk")
    even, odd = place
    return jnp.bitwise_xor(me, even if even == odd else jnp.where(me % 2 == 0, even, odd))


def weigh(places, k, doc_ref, square_ref, mask_ref, pieces, low_ref, window, add_degree, add_total):
    base, count, step = window
    features = doc_ref.shape[1]
    land_rows = pieces[0][0].shape[0]
    width = len(pieces) * land_rows
    scale = 4.0 / features * LOG2E
    col = lax.axis_index("col")
    cols = lax.axis_size("col")
    lands = jnp.concatenate(
        [
            jnp.concatenate([take(p, start, land_rows) for p in pieces], 1)
            for start in range(0, features, land_rows)
        ],
        0,
    )
    vectors = jnp.concatenate([take(p, features, k) for p in pieces], 0)
    wide = lands.astype(F32)
    land_square = scale * jnp.sum(wide * wide, 0, keepdims=True)
    live = mask_ref[...].astype(F32)
    lane = lax.broadcasted_iota(jnp.int32, live.shape, 1)
    line = lax.broadcasted_iota(jnp.int32, (live.shape[0], 1), 0)
    flags = [
        jnp.sum(jnp.where(lane == owner_of(place) * cols + col, live, 0.0), 1, keepdims=True)
        for place in places
    ]
    whole = pl.ds(base, count)
    prod = jnp.dot(doc_ref[whole, :], lands, preferred_element_type=F32)
    for start in range(0, count, step):
        rows, local = pl.ds(base + start, step), slice(start, start + step)
        block = (base + start) // BLOCK
        less = jnp.concatenate(
            [
                jnp.where(
                    jnp.sum(jnp.where(line == block, flag, 0.0), 0, keepdims=True) > 0.0,
                    land_square[:, n * land_rows : (n + 1) * land_rows],
                    DEAD,
                )
                for n, flag in enumerate(flags)
            ],
            1,
        )
        weights = jnp.exp2((2.0 * scale) * prod[local] - square_ref[rows, :][:, :1] - less)
        low_ref[local, :width] = weights.astype(BF16)
        part = weights[:, :128]
        for j in range(1, width // 128):
            part = part + weights[:, j * 128 : (j + 1) * 128]
        add_degree(rows, local, part)
    add_total(whole, jnp.dot(low_ref[:count, :width], vectors, preferred_element_type=F32))


def split_parts(places, refs):
    pieces = []
    for count, _ in places:
        pieces.append(refs[:count])
        refs = refs[count:]
    return pieces, refs


def first_kernel(places, doc_ref, mask_ref, *refs):
    pieces, (total_ref, degree_ref, square_ref, low_ref) = split_parts(places, refs)
    total_k = total_ref.shape[1]
    scale = 4.0 / doc_ref.shape[1] * LOG2E
    for i in range(doc_ref.shape[0] // BLOCK):
        rows = pl.ds(i * BLOCK, BLOCK)
        block = doc_ref[rows, :].astype(F32)
        total = scale * jnp.sum(block * block, 1, keepdims=True)
        square_ref[rows, :] = jnp.broadcast_to(total, (BLOCK, 128))

    def add_degree(rows, local, part):
        degree_ref[rows, :] = part

    def add_total(rows, part):
        total_ref[rows, :] = part

    window = 0, doc_ref.shape[0], BLOCK
    weigh([place for _, place in places], total_k, doc_ref, square_ref, mask_ref, pieces, low_ref, window, add_degree, add_total)


def more_kernel(places, doc_ref, square_ref, mask_ref, total_in, degree_in, *refs):
    pieces, (total_ref, degree_ref, low_ref) = split_parts(places, refs)
    total_k = total_ref.shape[1]

    def add_degree(rows, local, part):
        degree_ref[rows, :] = degree_in[rows, :] + part

    def add_total(rows, part):
        total_ref[rows, :] = total_in[rows, :] + part

    window = 0, doc_ref.shape[0], BLOCK
    weigh([place for _, place in places], total_k, doc_ref, square_ref, mask_ref, pieces, low_ref, window, add_degree, add_total)


def part_kernel(mask, places, doc_ref, square_ref, mask_ref, total_in, degree_in, *refs):
    pieces, refs = split_parts(places, refs)
    outs, (low_ref, part_ref) = refs[:-2], refs[-2:]
    n, k = low_ref.shape[0], total_in.shape[1]
    total_k = k
    step = math.gcd(n, BLOCK)
    base = pl.multiple_of(jnp.bitwise_xor(lax.axis_index("col"), mask) * n, step)
    totals = []

    def add_degree(rows, local, part):
        part_ref[local, :] = degree_in[rows, :] + part

    def add_total(rows, part):
        totals.append(total_in[rows, :] + part)

    window = base, n, step
    weigh([place for _, place in places], total_k, doc_ref, square_ref, mask_ref, pieces, low_ref, window, add_degree, add_total)
    deg = to_row(jnp.sum(part_ref[...], 1, keepdims=True), k)
    if mask == 0:
        outs[0][...] = totals[0]
        outs[1][...] = jnp.broadcast_to(deg, outs[1].shape)
    else:
        outs[0][:n, :] = totals[0].astype(BF16)
        high = deg.astype(BF16).astype(F32)
        spot = lax.broadcasted_iota(jnp.int32, (TAIL, k), 0)
        tail = jnp.where(spot == 0, high, jnp.where(spot == 1, deg - high, 0.0))
        outs[0][n:, :] = tail.astype(BF16)


def embed(own_ref, own_deg_ref, gets):
    n = own_ref.shape[0]
    proj = own_ref[...]
    deg = own_deg_ref[:1, :]
    for get in gets:
        proj = proj + get[:n, :].astype(F32)
        tail = get[n:, :].astype(F32)
        deg = deg + (tail[:1, :] + tail[1:2, :])
    return proj * lax.rsqrt(to_col(deg, n))


def embed_kernel(own_ref, own_deg_ref, *refs):
    refs[-1][...] = embed(own_ref, own_deg_ref, refs[:-1])


def hot_kernel(*refs):
    me = lax.axis_index("blk")
    chips = lax.axis_size("blk") // 2
    for label_ref, out in zip(refs[:2], refs[2:]):
        size, n = out.shape[0] // chips, out.shape[1]
        labels = jnp.broadcast_to(label_ref[...], (size, n))
        spot = lax.broadcasted_iota(jnp.int32, (size, n), 0)
        for chip in range(chips):
            owner = jnp.bitwise_xor(me, 2 * chip)
            hot = jnp.where(labels == spot + owner * size, 1.0, 0.0)
            out[chip * size : (chip + 1) * size, :] = hot.astype(BF16)


def add_rows(hot, high, low):
    return jnp.dot(hot, high, preferred_element_type=F32) + jnp.dot(hot, low, preferred_element_type=F32)


def norm_kernel(own_ref, own_deg_ref, *refs):
    high_ref, low_ref = refs[-2:]
    emb = embed(own_ref, own_deg_ref, refs[:-2])
    unit = emb * lax.rsqrt(jnp.sum(emb * emb, 1, keepdims=True) + 1e-06)
    high = unit.astype(BF16)
    low = (unit - high.astype(F32)).astype(BF16)
    high_ref[...] = high
    low_ref[...] = low


def keep_kernel(hot_ref, high_ref, low_ref, keep_ref):
    keep_ref[...] = add_rows(hot_ref[...], high_ref[...], low_ref[...])


def split_kernel(keep_ref, hot_ref, get_ref, own_ref, *sends):
    size = own_ref.shape[0]
    both = keep_ref[...] + jnp.dot(hot_ref[...], get_ref[...], preferred_element_type=F32)
    for chip, out in enumerate((own_ref, *sends)):
        out[...] = both[chip * size : (chip + 1) * size].astype(out.dtype)


def tree(parts):
    while len(parts) > 1:
        parts = [a + b for a, b in zip(parts[::2], parts[1::2])]
    return parts[0]


def sum_kernel(*refs):
    refs[-1][...] = tree([ref[...].astype(F32) for ref in refs[:-1]]).astype(refs[-1].dtype)


def place_kernel(places, aliased, *refs):
    parts, (out_hbm, wide_ref, sem) = refs[: len(places)], refs[-3:]
    del aliased
    size = parts[0].shape[0]
    count = out_hbm.shape[0]
    whole, rest = count // size, count % size
    copies = []
    for n, (place, part) in enumerate(zip(places, parts)):
        owner = jnp.bitwise_xor(lax.axis_index("blk"), place)
        wide_ref[n] = part[...].astype(F32)
        full = pltpu.make_async_copy(
            wide_ref.at[n],
            out_hbm.at[pl.ds(pl.multiple_of(jnp.minimum(owner, whole - 1) * size, 8), size), :],
            sem.at[n],
        )
        copies.append((owner < whole, full))
        if rest:
            end = pltpu.make_async_copy(
                wide_ref.at[n, pl.ds(0, rest), :], out_hbm.at[pl.ds(whole * size, rest), :], sem.at[n]
            )
            copies.append((owner == whole, end))
    for here, copy in copies:
        pl.when(here)(copy.start)
    for here, copy in copies:
        pl.when(here)(copy.wait)


def body(documents, landmarks, eigen_vectors, land_degree, eigen_values, tile_mask, labels):
    blks, cols = lax.axis_size("blk"), lax.axis_size("col")
    chips = blks // 2
    doc_rows, features = documents.shape
    land_rows = landmarks.shape[0]
    k = eigen_vectors.shape[1]
    rows = doc_rows // cols
    assert rows <= k and doc_rows % BLOCK == 0 and land_rows == BLOCK and features % BLOCK == 0

    def swap(x, pick):
        return lax.ppermute(x, "blk", [(i, pick(i)) for i in range(blks)])

    def core_swap(x):
        return swap(x, lambda i: i ^ 1)

    def chip_swap(x, mask):
        return swap(x, lambda i: i ^ (2 * mask))

    def col_swap(x, mask):
        return lax.ppermute(x, "col", [(i, i ^ mask) for i in range(cols)])

    spot = call(spot_kernel, [struct((8, land_rows), jnp.int32)], [], flops=HEAVY)[0]
    width = features + k
    split_a = chips == 4 and width % (2 * land_rows) == 0 and features * 2 >= width
    half = [struct((land_rows, width // 2), BF16)] * 2 if split_a else []
    own, *halves = call(
        prep_kernel,
        [struct((land_rows, width), BF16)] + half,
        [spot, landmarks, eigen_vectors, land_degree.reshape(1, -1), eigen_values.reshape(1, -1)],
        flops=HEAVY,
    )

    if chips == 4:
        step_a = lambda i: i ^ 2 if i % 2 == 0 else i ^ 4
        step_b = lambda i: i ^ 4 if i % 2 == 0 else i ^ 2
        got_a = [swap(x, step_a) for x in halves or [own]]
        got_b = swap(own, step_b)
        got_f = [swap(x, step_b) for x in got_a]
        far_own, far_b = core_swap(own), core_swap(got_b)
        far_a = [core_swap(x) for x in got_a]
        far_f = [core_swap(x) for x in got_f]
        groups = [
            [([own], (0, 0)), ([far_own], (1, 1))],
            [(got_a, (2, 4)), (far_a, (5, 3))],
            [([got_b], (4, 2)), ([far_b], (3, 5))],
            [(got_f, (6, 6)), (far_f, (7, 7))],
        ]
    else:
        near = [own] + [chip_swap(own, mask) for mask in range(1, chips)]
        groups = [
            [([x], (2 * mask, 2 * mask)), ([core_swap(x)], (2 * mask + 1, 2 * mask + 1))]
            for mask, x in enumerate(near)
        ]

    scratch = [pltpu.VMEM((doc_rows, 2 * land_rows), BF16)]
    sums = [struct((doc_rows, k), F32), struct((doc_rows, 128), F32)]

    def run(kernel, group, outs, args, scratch, aliases=None, share=1):
        places = [(len(parts), place) for parts, place in group]
        args = args + [part for parts, _ in group for part in parts]
        flops = len(group) * 2 * doc_rows * land_rows * (features + k) // share
        kernel = functools.partial(kernel, places)
        return call(kernel, outs, args, None, scratch, flops, aliases=aliases)

    *state, square = run(first_kernel, groups[0], sums + sums[1:], [documents, tile_mask], scratch)
    head = [documents, square, tile_mask]
    for group in groups[1:-1]:
        state = run(more_kernel, group, sums, head + list(state), scratch, {3: 0, 4: 1})
    narrow = [pltpu.VMEM((rows, len(groups[-1]) * land_rows), BF16), pltpu.VMEM((rows, 128), F32)]

    def part(mask, outs):
        kernel = functools.partial(part_kernel, mask)
        return run(kernel, groups[-1], outs, head + list(state), narrow, share=cols)

    parts = part(0, [struct((rows, k), F32), struct((8, k), F32)])
    sends = [part(mask, [struct((rows + TAIL, k), BF16)])[0] for mask in range(1, cols)]
    gets = [col_swap(x, mask + 1) for mask, x in enumerate(sends)]
    size = -(-(-(-C // blks)) // 16) * 16
    names = labels.reshape(1, -1)
    wide = struct((chips * size, k), F32)
    unit = struct((rows, k), BF16)
    hot = struct((chips * size, rows), BF16)
    far_names = core_swap(names)
    hot_keep, hot_far = call(hot_kernel, [hot, hot], [names, far_names])
    high, low = call(norm_kernel, [unit, unit], [parts[0], parts[1], *gets])
    get = core_swap(high)
    keep = call(keep_kernel, [wide], [hot_keep, high, low])[0]
    embedding = call(embed_kernel, [struct((rows, k), F32)], [parts[0], parts[1], *gets])[0]
    one, low = struct((size, k), F32), struct((size, k), BF16)
    split = call(split_kernel, [one] + [low] * (chips - 1), [keep, hot_far, get])
    gets = [chip_swap(x, mask + 1) for mask, x in enumerate(split[1:])]
    mine = call(sum_kernel, [low], [split[0], *gets])[0]
    gets = [col_swap(mine, mask) for mask in range(1, cols)]
    done = call(sum_kernel, [low], [mine, *gets])[0]
    near = [done] + [chip_swap(done, mask) for mask in range(1, chips)]
    far = [core_swap(x) for x in near]
    centroids = None
    hbm = pl.BlockSpec(memory_space=pl.ANY)
    for core, chunks in enumerate((near, far)):
        extra = [] if centroids is None else [centroids]
        centroids = call(
            functools.partial(place_kernel, [2 * mask + core for mask in range(chips)], bool(extra)),
            [struct((C, k), F32)],
            chunks + extra,
            [VMEM] * chips + [hbm] * len(extra),
            [pltpu.VMEM((chips, size, k), F32), pltpu.SemaphoreType.DMA((chips,))],
            aliases={chips: 0} if extra else None,
            out_specs=[hbm],
        )[0]
    return (embedding, centroids)


def solution(mesh):
    placed = (
        P("blk", None),
        P(("blk", "col"), None),
        P(("blk", "col"), None),
        P(("blk", "col")),
        P(),
        P("blk", None),
        P(("blk", "col")),
    )

    return jax.shard_map(body, mesh=mesh, in_specs=placed, out_specs=(P(("blk", "col"), None), P()), check_vma=False)
```
